128 devices in a mesh: row: 8 (over z_lo, x), col: 16 (over y, z_hi, core).
Axes of the slice: x: 4, y: 4, z: 4 (z_hi: 2, z_lo: 2; z = z_hi * 2 + z_lo), core: 2. Of those that a mesh axis runs over, the one named last changes fastest.
Arguments:
- features: bfloat16 [16, 256, 64, 1024], P('row', 'col'), may hold values from -6 to 6
- tissue: int32 [16, 256, 64], P('row', 'col'), may hold values 0 or 1
- probe: float32 [16, 256, 4096], P('row', 'col'), may hold values from -6 to 6
Outputs:
- basis: float32 [16, 256, 4096], P('row', 'col')
The draws below stay inside these ranges and needn't reach their ends.
All inputs are finite; a program needn't handle non-finite values. No bound on the sum of `tissue` on one device may be relied on, other than what follows from the above.
Results may differ from the reference program's by a relative error of at most 0.00091.
Values may be sent and summed in bfloat16 or wider, within the bound.
A program may use at most 128 MiB of HBM per device.

```python
import math
import jax
import jax.numpy as jnp
from jax import lax

D = 1024
PATCH = 64
RANK = 64
ITERS = 3
NR = 16
NC = 256


def with_ends(values, rng, low, high):
    spot = [jax.random.randint(jax.random.fold_in(rng, axis), (), 0, length) for axis, length in enumerate(values.shape)]
    main_axis = values.shape.index(max(values.shape))
    next_to = spot[:main_axis] + [(spot[main_axis] + 1) % values.shape[main_axis]] + spot[main_axis + 1:]
    return values.at[tuple(spot)].set(low).at[tuple(next_to)].set(high)


def block_scale(rng, extent, pieces, least, top_value):
    loudness = 1.0
    for dim, blocks in pieces:
        draws = jax.random.uniform(jax.random.fold_in(jax.random.fold_in(rng, 6), dim), (blocks,), jnp.float32, least / len(pieces), top_value / len(pieces))
        loudness = loudness * jnp.repeat(jnp.exp(draws), extent[dim] // blocks).reshape((-1,) + (1,) * (len(extent) - 1 - dim))
    return loudness


def centred(own_key, extent, spread, most, split=(), kind=jnp.bfloat16):
    level = block_scale(own_key, extent, split, -0.22, 0.18) if split else 1.0
    drawn = jax.random.normal(own_key, extent, jnp.float32) * spread * level
    return jnp.minimum(jnp.maximum(drawn, -most), most).astype(kind)


def setup_inputs(seed: int = 0) -> dict:
    key_of = jax.random.split(jax.random.key(seed), 4)
    features = centred(key_of[0], (NR, NC, PATCH, D), 1.0, 6.0, ((0, 8), (1, 16)))
    tissue = with_ends((jax.random.randint(key_of[1], (NR, NC, PATCH), 0, 4) < 3).astype(jnp.int32), jax.random.fold_in(key_of[1], 1), 0, 1)
    probe = centred(key_of[2], (NR, NC, PATCH * RANK), 1.0, 6.0, ((0, 8), (1, 16)), jnp.float32)
    return dict(features=features, tissue=tissue, probe=probe)


AFFINITY_TEMP = 4.0

def normalized(features):
    values = features.astype(jnp.float32)
    scaled = values * lax.rsqrt(lax.optimization_barrier(jnp.sum(values * values, axis=-1, keepdims=True)) + 1e-06)
    return scaled.astype(jnp.bfloat16)

def reference(features, tissue, probe):
    unit = normalized(features)
    tissue_float = tissue.astype(jnp.float32)
    padded = jnp.pad(unit, ((1, 1), (1, 1), (0, 0), (0, 0)))
    padded_mask = jnp.pad(tissue_float, ((1, 1), (1, 1), (0, 0)))

    def tile_row(start):
        rows = lax.dynamic_slice_in_dim(padded, start, 3, 0).astype(jnp.float32)
        masks = lax.dynamic_slice_in_dim(padded_mask, start, 3, 0)
        centre = rows[1, 1:NC + 1]
        central_mask = masks[1, 1:NC + 1]
        blocks = []
        for shift_row in range(3):
            for shift_col in range(3):
                other = rows[shift_row, shift_col:shift_col + NC]
                neighbour_mask = masks[shift_row, shift_col:shift_col + NC]
                affinity_scores = jnp.einsum('cpd,cqd->cpq', centre, other, precision=lax.Precision.HIGHEST)
                affinity_weights = central_mask[:, :, None] * neighbour_mask[:, None, :] * jnp.exp(AFFINITY_TEMP * (affinity_scores - 1.0))
                blocks.append(affinity_weights)
        return jnp.concatenate(blocks, axis=2)
    affinity = lax.map(tile_row, jnp.arange(NR, dtype=jnp.int32))
    degree = 1.0 + lax.optimization_barrier(jnp.sum(affinity, axis=-1))
    inverse_root = lax.rsqrt(degree)
    panel = probe.reshape(NR, NC, PATCH, RANK)
    for step in range(ITERS):
        carried = inverse_root[..., None] * panel
        padded_panel = jnp.pad(carried, ((1, 1), (1, 1), (0, 0), (0, 0)))
        summed = jnp.zeros((NR, NC, PATCH, RANK), jnp.float32)
        for shift_row in range(3):
            for shift_col in range(3):
                which = 3 * shift_row + shift_col
                block = affinity[:, :, :, which * PATCH:(which + 1) * PATCH]
                source = padded_panel[shift_row:shift_row + NR, shift_col:shift_col + NC]
                summed = summed + jnp.einsum('abpq,abqk->abpk', block, source, precision=lax.Precision.HIGHEST)
        image = panel + inverse_root[..., None] * summed
        flat = image.reshape(-1, RANK)
        gram_matrix = jnp.dot(flat.T.astype(jnp.float32), flat.astype(jnp.float32), precision=lax.Precision.HIGHEST, preferred_element_type=jnp.float32)
        lower = jnp.linalg.cholesky(gram_matrix)
        solved = jax.scipy.linalg.solve_triangular(lower, flat.T, lower=True)
        panel = solved.T.reshape(NR, NC, PATCH, RANK)
    factor = math.sqrt(float(NR * NC * PATCH))
    return (factor * panel).reshape(NR, NC, PATCH * RANK)
```

```python
import functools
import math

import jax
import jax.numpy as jnp
from jax import lax
from jax.experimental import pallas as pl
from jax.experimental.pallas import tpu as pltpu
from jax.sharding import Mesh
from jax.sharding import PartitionSpec as P

RANK = 64
ITERS = 3
PATCH = 64
AXES = ("row_0", "row_1", "col_0", "col_1", "col_2")
ROW = ("row_0", "row_1")
COL = ("col_0", "col_1", "col_2")
NROW, NCOL = 8, 16
TC = 16
MESH_ID = pl.DeviceIdType.MESH
AFFINITY_TEMP = 4.0
STEPS = 8
WIDTH = TC // STEPS

DIRS = ((-1, 0), (1, 0), (0, -1), (0, 1), (-1, -1), (-1, 1), (1, -1), (1, 1))


def position():
    return tuple(lax.axis_index(a) for a in AXES)


def row_col(pos):
    return pos[0] * 4 + pos[1], pos[2] * 4 + pos[3] * 2 + pos[4]


def device_at(row, col):
    row = jnp.clip(row, 0, NROW - 1)
    col = jnp.clip(col, 0, NCOL - 1)
    return (row // 4, row % 4, col // 4, (col // 2) % 2, col % 2)


def inside(row, col):
    return (row >= 0) & (row < NROW) & (col >= 0) & (col < NCOL)


def barrier(row, col, others):
    sem = pltpu.get_barrier_semaphore()
    for dr, dc in DIRS:

        @pl.when(inside(row + dr, col + dc))
        def _(dr=dr, dc=dc):
            pl.semaphore_signal(
                sem, inc=1, device_id=device_at(row + dr, col + dc), device_id_type=MESH_ID
            )

    for other in others:
        pl.semaphore_signal(sem, inc=1, device_id=other, device_id_type=MESH_ID)
    near = sum(inside(row + dr, col + dc).astype(jnp.int32) for dr, dc in DIRS)
    pl.semaphore_wait(sem, near + len(others))


def send_slices(dr, dc, first=1, count=TC):
    if dc == 0:
        src, dst = pl.ds(first, count), pl.ds(first, count)
    elif dc < 0:
        src, dst = pl.ds(1, 1), pl.ds(TC + 1, 1)
    else:
        src, dst = pl.ds(TC, 1), pl.ds(0, 1)
    return src, dst


def halo_copy(own, halo, dr, dc, send, recv, device, first=1, count=TC):
    src, dst = send_slices(dr, dc, first, count)
    if dr == 0:
        a, b = own.at[src], own.at[dst]
    elif dr < 0:
        a, b = own.at[src, 0:PATCH], halo.at[dst, PATCH : 2 * PATCH]
    else:
        a, b = own.at[src, PATCH : 2 * PATCH], halo.at[dst, 0:PATCH]
    return pltpu.make_async_remote_copy(
        src_ref=a, dst_ref=b, send_sem=send, recv_sem=recv, device_id=device, device_id_type=MESH_ID
    )


def mask_copy(mask, dr, dc, send, recv, device):
    src, dst = send_slices(dr, dc)
    if dr == 0:
        a, b = mask.at[0:2, src], mask.at[0:2, dst]
    elif dr < 0:
        a, b = mask.at[0:1, src], mask.at[3:4, dst]
    else:
        a, b = mask.at[1:2, src], mask.at[2:3, dst]
    return pltpu.make_async_remote_copy(
        src_ref=a, dst_ref=b, send_sem=send, recv_sem=recv, device_id=device, device_id_type=MESH_ID
    )


NT = (((1,), (1,)), ((), ()))
TN = (((0,), (0,)), ((), ()))


def eye(n):
    return lax.broadcasted_iota(jnp.int32, (n, n), 0) == lax.broadcasted_iota(jnp.int32, (n, n), 1)


def affinity_kernel(
    feat, tissue, e_ref, aux_ref, own, halo, mask, deg, usend, urecv, csend, crecv, msend, mrecv
):
    row, col = row_col(position())

    for k in (2, 3):
        mask[k] = jnp.zeros((TC + 2, 8, 128), jnp.float32)
    for k in (0, 1):
        mask[k, 0] = jnp.zeros((8, 128), jnp.float32)
        mask[k, TC + 1] = jnp.zeros((8, 128), jnp.float32)
        t = tissue[k].astype(jnp.float32)
        t = jnp.concatenate([t, t], axis=1)
        for c in range(TC):
            mask[k, c + 1] = jnp.broadcast_to(t[c : c + 1, :], (8, 128))

    barrier(row, col, ())

    def edges(step, fn):
        first = 1 + step * WIDTH
        for k in (0, 1):
            dr = DIRS[k][0]
            fn(
                k,
                halo_copy(
                    own, halo, dr, 0, usend.at[k, step], urecv.at[k, step],
                    device_at(row + dr, col), first, WIDTH,
                ),
            )

    def start_edges(step):
        def go(k, copy):
            @pl.when(inside(row + DIRS[k][0], col))
            def _():
                copy.start()

        edges(step, go)

    def normalise(c):
        for k in (0, 1):
            v = feat[k, c].astype(jnp.float32)
            total = jnp.sum(v * v, axis=-1, keepdims=True)
            own[c + 1, k * PATCH : (k + 1) * PATCH] = (v * lax.rsqrt(total + 1e-06)).astype(
                jnp.bfloat16
            )

    for c in range(WIDTH):
        normalise(c)

    def group(step, _):
        for i in range(WIDTH):
            normalise(step * WIDTH + i)
        start_edges(step - 1)
        return 0

    lax.fori_loop(1, STEPS, group, 0)
    start_edges(STEPS - 1)

    def side(k):
        dr, dc = DIRS[k]
        device = device_at(row + dr, col + dc)
        return halo_copy(own, halo, dr, dc, csend.at[k], crecv.at[k], device)

    def side_mask(k):
        dr, dc = DIRS[k]
        device = device_at(row + dr, col + dc)
        return mask_copy(mask, dr, dc, msend.at[k], mrecv.at[k], device)

    for k, (dr, dc) in enumerate(DIRS):

        @pl.when(inside(row + dr, col + dc))
        def _(k=k):
            side_mask(k).start()
            if k >= 2:
                side(k).start()

    lane = lax.broadcasted_iota(jnp.int32, (128, 128), 1)
    sub = lax.broadcasted_iota(jnp.int32, (128, 128), 0)
    diagonal = lane == sub
    seen = (lane < PATCH) == (sub < PATCH)

    def block(c, cc, other, upper, lower, kind):
        s = lax.dot_general(own[c], other[cc], NT, preferred_element_type=jnp.float32)
        w = jnp.exp(AFFINITY_TEMP * (s - 1.0))
        m = jnp.where(lane[0:1] < PATCH, upper[cc, 0:1], lower[cc, 0:1])
        keep = jnp.broadcast_to(m, (128, 128)) > 0.5
        if kind == 1:
            keep = keep & seen
        return jnp.where(keep, w, 0.0)

    def own_blocks(c, parts):
        total = jnp.zeros((128, 1), jnp.float32)
        for d in parts:
            w = block(c, c + d - 1, own, mask.at[0], mask.at[1], 0)
            total = total + jnp.sum(w, axis=1, keepdims=True)
            if d == 1:
                self_w = jnp.sum(jnp.where(diagonal, w, 0.0), axis=1, keepdims=True)
                aux_ref[c - 1, :, 64:128] = jnp.broadcast_to(self_w, (128, 64))
                w = jnp.where(diagonal, 0.0, w)
            e_ref[c - 1, 0, :, d * 128 : (d + 1) * 128] = w.astype(jnp.bfloat16)
        return total

    def halo_blocks(c):
        total = jnp.zeros((128, 1), jnp.float32)
        for d in range(3):
            w = block(c, c + d - 1, halo, mask.at[2], mask.at[3], 1)
            total = total + jnp.sum(w, axis=1, keepdims=True)
            e_ref[c - 1, 1, :, d * 128 : (d + 1) * 128] = w.astype(jnp.bfloat16)
        return total

    def inner(c, _):
        deg[c] = jnp.broadcast_to(own_blocks(c, (0, 1, 2)), (128, 128))
        return 0

    lax.fori_loop(2, TC, inner, 0)

    for k, (dr, dc) in enumerate(DIRS):

        @pl.when(inside(row - dr, col - dc))
        def _(k=k):
            side_mask(k).wait_recv()
            if k >= 2:
                side(k).wait_recv()

    for c in (1, TC):
        deg[c] = jnp.broadcast_to(own_blocks(c, (0, 1, 2)), (128, 128))

    def finish(c):
        total = deg[c][:, 0:1] + halo_blocks(c)
        m = jnp.where(lane[0:1] < PATCH, mask[0, c, 0:1], mask[1, c, 0:1])
        mine = jnp.sum(jnp.where(diagonal, jnp.broadcast_to(m, (128, 128)), 0.0), axis=1, keepdims=True)
        scale = lax.rsqrt(1.0 + mine * total)
        self_w = aux_ref[c - 1, :, 64:65]
        aux_ref[c - 1, :, 0:64] = jnp.broadcast_to(scale, (128, 64))
        aux_ref[c - 1, :, 64:128] = jnp.broadcast_to(scale * mine, (128, 64))
        deg[c] = jnp.broadcast_to(1.0 + mine * scale * scale * self_w, (128, 128))

    def wait_edges(step):
        def go(k, copy):
            @pl.when(inside(row - DIRS[k][0], col))
            def _():
                copy.wait_recv()

        edges(step, go)

    wait_edges(0)
    for c in range(1, WIDTH):
        finish(c)

    def halo_group(step, _):
        wait_edges(step)
        for i in range(WIDTH):
            finish(step * WIDTH + i)
        return 0

    lax.fori_loop(1, STEPS, halo_group, 0)
    finish(TC)

    def drain(step, _):
        def go(k, copy):
            @pl.when(inside(row + DIRS[k][0], col))
            def _():
                copy.wait_send()

        edges(step, go)
        return 0

    lax.fori_loop(0, STEPS, drain, 0)
    for k, (dr, dc) in enumerate(DIRS):

        @pl.when(inside(row + dr, col + dc))
        def _(k=k):
            side_mask(k).wait_send()
            if k >= 2:
                side(k).wait_send()

    return deg


def affinity_body(
    feat, tissue, e_ref, aux_ref, diag_ref, own, halo, mask, deg, *sems
):
    affinity_kernel(feat, tissue, e_ref, aux_ref, own, halo, mask, deg, *sems)

    def put(c, _):
        diag_ref[c] = deg[c + 1][:, 0:64]
        return 0

    lax.fori_loop(0, TC, put, 0)


def stage_peers(pos):
    z = pos[3] * 2 + pos[0]
    core = (pos[4], [(pos[0], pos[1], pos[2], pos[3], 1 - pos[4])])
    x = (pos[1], [(pos[0], (pos[1] + d) % 4, pos[2], pos[3], pos[4]) for d in (1, 2, 3)])
    y = (pos[2], [(pos[0], pos[1], (pos[2] + d) % 4, pos[3], pos[4]) for d in (1, 2, 3)])
    along = [(z + d) % 4 for d in (1, 2, 3)]
    zz = (z, [(q % 2, pos[1], pos[2], q // 2, pos[4]) for q in along])
    return [core, x, y, zz]


def hi_lo(v):
    hi = v.astype(jnp.bfloat16)
    lo = (v - hi.astype(jnp.float32)).astype(jnp.bfloat16)
    return jnp.concatenate([hi, lo], axis=1)


def inverse_factor(gram):
    n = RANK
    m = jnp.concatenate([gram, jnp.where(eye(n), 1.0, 0.0)], axis=1)
    sub = lax.broadcasted_iota(jnp.int32, (n, 2 * n), 0)
    lane = lax.broadcasted_iota(jnp.int32, (n, 2 * n), 1)
    for k in range(n - 1):
        column = jnp.broadcast_to(m[:, k : k + 1], (n, 2 * n))
        pivot = column[k : k + 1, :]
        line = m[k : k + 1, :] / pivot
        m = m - jnp.where(sub > k, column, 0.0) * line
    d = jnp.sum(jnp.where(lane == sub, m, 0.0), axis=1, keepdims=True)
    return m[:, n:] * lax.rsqrt(d)


def iterate_kernel(
    e_ref, aux_ref, diag_ref, probe_ref, out_ref,
    own, halo, acc, q, pair, total, gsum, psend, precv, gsend, grecv,
):
    pos = position()
    row, col = row_col(pos)
    stages = stage_peers(pos)

    zero = jnp.zeros((128, 128), jnp.bfloat16)

    def clear(i, _):
        own[i, 0] = zero
        own[i, TC + 1] = zero

        def one(c, _):
            halo[i, c] = zero
            return 0

        lax.fori_loop(0, TC + 2, one, 0)
        return 0

    lax.fori_loop(0, ITERS, clear, 0)

    def load(c, _):
        v = probe_ref[c]
        q[c] = v
        own[0, c + 1] = hi_lo(v * aux_ref[c, :, 0:64])
        return 0

    lax.fori_loop(0, TC, load, 0)
    barrier(row, col, [p for _, peers in stages for p in peers])

    def step(t, _):
        def panel(k):
            dr, dc = DIRS[k]
            return halo_copy(
                own.at[t], halo.at[t], dr, dc, psend.at[t, k], precv.at[t, k],
                device_at(row + dr, col + dc),
            )

        for k, (dr, dc) in enumerate(DIRS):

            @pl.when(inside(row + dr, col + dc))
            def _(k=k):
                panel(k).start()

        def own_part(c, _):
            b = own[t, pl.ds(c, 3)].reshape(384, 128)
            acc[c] = jnp.dot(e_ref[c, 0], b, preferred_element_type=jnp.float32)
            return 0

        lax.fori_loop(1, TC - 1, own_part, 0)
        for k, (dr, dc) in enumerate(DIRS):

            @pl.when(inside(row - dr, col - dc))
            def _(k=k):
                panel(k).wait_recv()

        own_part(0, 0)
        own_part(TC - 1, 0)
        total[...] = jnp.zeros((128, 128), jnp.float32)

        def halo_part(c, _):
            b = halo[t, pl.ds(c, 3)].reshape(384, 128)
            v = acc[c] + jnp.dot(e_ref[c, 1], b, preferred_element_type=jnp.float32)
            v = v[:, :64] + v[:, 64:]
            y = q[c] * diag_ref[c] + aux_ref[c, :, 64:128] * v
            p = hi_lo(y)
            pair[c] = p
            total[...] += lax.dot_general(p, p, TN, preferred_element_type=jnp.float32)
            return 0

        lax.fori_loop(0, TC, halo_part, 0)
        g = total[...]
        g = g[:, :64] + g[:, 64:]
        g = g[:64] + g[64:]
        packed = jnp.concatenate([g[:32], g[32:]], axis=1)

        for s, (place, peers) in enumerate(stages):
            n = len(peers) + 1
            gsum[t, s, place] = packed

            def exchange(d, there, s=s, place=place, n=n):
                return pltpu.make_async_remote_copy(
                    src_ref=gsum.at[t, s, place],
                    dst_ref=gsum.at[t, s, place],
                    send_sem=gsend.at[t, s, d],
                    recv_sem=grecv.at[t, s, d],
                    device_id=there,
                    device_id_type=MESH_ID,
                )

            def arrival(d, there, s=s, place=place, n=n):
                origin = (place + n - 1 - d) % n
                return pltpu.make_async_remote_copy(
                    src_ref=gsum.at[t, s, place],
                    dst_ref=gsum.at[t, s, origin],
                    send_sem=gsend.at[t, s, d],
                    recv_sem=grecv.at[t, s, d],
                    device_id=there,
                    device_id_type=MESH_ID,
                )

            for d, there in enumerate(peers):
                exchange(d, there).start()
            for d, there in enumerate(peers):
                arrival(d, there).wait_recv()
            packed = gsum[t, s, 0]
            for i in range(1, n):
                packed = packed + gsum[t, s, i]

        gram = jnp.concatenate([packed[:, :64], packed[:, 64:]], axis=0)
        inv = inverse_factor(gram)
        hi = inv.astype(jnp.bfloat16)
        lo = (inv - hi.astype(jnp.float32)).astype(jnp.bfloat16)
        both = jnp.concatenate(
            [jnp.concatenate([hi, hi], axis=1), jnp.concatenate([lo, lo], axis=1)], axis=0
        )

        def solve(c):
            v = lax.dot_general(pair[c], both, NT, preferred_element_type=jnp.float32)
            return v[:, :64] + v[:, 64:]

        @pl.when(t < ITERS - 1)
        def _():
            def renew(c, _):
                v = solve(c)
                q[c] = v
                own[t + 1, c + 1] = hi_lo(v * aux_ref[c, :, 0:64])
                return 0

            lax.fori_loop(0, TC, renew, 0)

        @pl.when(t == ITERS - 1)
        def _():
            factor = math.sqrt(float(NROW * 2 * NCOL * TC * PATCH))

            def last(c, _):
                out_ref[c] = factor * solve(c)
                return 0

            lax.fori_loop(0, TC, last, 0)

        for k, (dr, dc) in enumerate(DIRS):

            @pl.when(inside(row + dr, col + dc))
            def _(k=k):
                panel(k).wait_send()

        for s, (place, peers) in enumerate(stages):
            for d, there in enumerate(peers):
                pltpu.make_async_remote_copy(
                    src_ref=gsum.at[t, s, place],
                    dst_ref=gsum.at[t, s, place],
                    send_sem=gsend.at[t, s, d],
                    recv_sem=grecv.at[t, s, d],
                    device_id=there,
                    device_id_type=MESH_ID,
                ).wait_send()
        return 0

    lax.fori_loop(0, ITERS, step, 0)


VM = pl.BlockSpec(memory_space=pltpu.VMEM)
DMA = pltpu.SemaphoreType.DMA
LIMIT = 60 * 2**20


def local(features, tissue, probe):
    width = features.shape[-1]
    e, aux, diag = pl.pallas_call(
        affinity_body,
        out_shape=(
            jax.ShapeDtypeStruct((TC, 2, 128, 384), jnp.bfloat16),
            jax.ShapeDtypeStruct((TC, 128, 128), jnp.float32),
            jax.ShapeDtypeStruct((TC, 128, 64), jnp.float32),
        ),
        in_specs=[VM, VM],
        out_specs=(VM, VM, VM),
        scratch_shapes=[
            pltpu.VMEM((TC + 2, 128, width), jnp.bfloat16),
            pltpu.VMEM((TC + 2, 128, width), jnp.bfloat16),
            pltpu.VMEM((4, TC + 2, 8, 128), jnp.float32),
            pltpu.VMEM((TC + 1, 128, 128), jnp.float32),
            DMA((2, STEPS)), DMA((2, STEPS)), DMA((8,)), DMA((8,)), DMA((8,)), DMA((8,)),
        ],
        compiler_params=pltpu.CompilerParams(
            collective_id=0, has_side_effects=True, vmem_limit_bytes=LIMIT
        ),
        name="affinity",
    )(features, tissue)
    panel = probe.reshape(2, TC, PATCH, RANK).transpose(1, 0, 2, 3).reshape(TC, 128, RANK)
    out = pl.pallas_call(
        iterate_kernel,
        out_shape=jax.ShapeDtypeStruct((TC, 128, RANK), jnp.float32),
        in_specs=[VM] * 4,
        out_specs=VM,
        scratch_shapes=[
            pltpu.VMEM((ITERS, TC + 2, 128, 128), jnp.bfloat16),
            pltpu.VMEM((ITERS, TC + 2, 128, 128), jnp.bfloat16),
            pltpu.VMEM((TC, 128, 128), jnp.float32),
            pltpu.VMEM((TC, 128, RANK), jnp.float32),
            pltpu.VMEM((TC, 128, 128), jnp.bfloat16),
            pltpu.VMEM((128, 128), jnp.float32),
            pltpu.VMEM((ITERS, 4, 4, 32, 128), jnp.float32),
            DMA((ITERS, 8)), DMA((ITERS, 8)), DMA((ITERS, 4, 3)), DMA((ITERS, 4, 3)),
        ],
        compiler_params=pltpu.CompilerParams(
            collective_id=1, has_side_effects=True, vmem_limit_bytes=LIMIT
        ),
        name="iterate",
    )(e, aux, diag, panel)
    return out.reshape(TC, 2, PATCH, RANK).transpose(1, 0, 2, 3).reshape(2, TC, PATCH * RANK)


def solution(mesh):
    torus = Mesh(mesh.devices.reshape(2, 4, 4, 2, 2), AXES)
    return jax.shard_map(
        local,
        mesh=torus,
        in_specs=(P(ROW, COL, None, None), P(ROW, COL, None), P(ROW, COL, None)),
        out_specs=P(ROW, COL, None),
        check_vma=False,
    )
```

```python
import functools
import math

import jax
import jax.numpy as jnp
from jax import lax
from jax.experimental import pallas as pl
from jax.experimental.pallas import tpu as pltpu
from jax.sharding import Mesh
from jax.sharding import PartitionSpec as P

RANK = 64
ITERS = 3
PATCH = 64
AXES = ("row_0", "row_1", "col_0", "col_1", "col_2")
ROW = ("row_0", "row_1")
COL = ("col_0", "col_1", "col_2")
NROW, NCOL = 8, 16
TC = 16
MESH_ID = pl.DeviceIdType.MESH
AFFINITY_TEMP = 4.0
STEPS = 8
WIDTH = TC // STEPS

DIRS = ((-1, 0), (1, 0), (0, -1), (0, 1), (-1, -1), (-1, 1), (1, -1), (1, 1))


def position():
    return tuple(lax.axis_index(a) for a in AXES)


def row_col(pos):
    return pos[0] * 4 + pos[1], pos[2] * 4 + pos[3] * 2 + pos[4]


def device_at(row, col):
    row = jnp.clip(row, 0, NROW - 1)
    col = jnp.clip(col, 0, NCOL - 1)
    return (row // 4, row % 4, col // 4, (col // 2) % 2, col % 2)


def inside(row, col):
    return (row >= 0) & (row < NROW) & (col >= 0) & (col < NCOL)


def barrier(row, col, others):
    sem = pltpu.get_barrier_semaphore()
    for dr, dc in DIRS:

        @pl.when(inside(row + dr, col + dc))
        def _(dr=dr, dc=dc):
            pl.semaphore_signal(
                sem, inc=1, device_id=device_at(row + dr, col + dc), device_id_type=MESH_ID
            )

    for other in others:
        pl.semaphore_signal(sem, inc=1, device_id=other, device_id_type=MESH_ID)
    near = sum(inside(row + dr, col + dc).astype(jnp.int32) for dr, dc in DIRS)
    pl.semaphore_wait(sem, near + len(others))


def send_slices(dr, dc, first=1, count=TC):
    if dc == 0:
        src, dst = pl.ds(first, count), pl.ds(first, count)
    elif dc < 0:
        src, dst = pl.ds(1, 1), pl.ds(TC + 1, 1)
    else:
        src, dst = pl.ds(TC, 1), pl.ds(0, 1)
    return src, dst


def halo_copy(own, halo, dr, dc, send, recv, device, first=1, count=TC):
    src, dst = send_slices(dr, dc, first, count)
    if dr == 0:
        a, b = own.at[src], own.at[dst]
    elif dr < 0:
        a, b = own.at[src, 0:PATCH], halo.at[dst, PATCH : 2 * PATCH]
    else:
        a, b = own.at[src, PATCH : 2 * PATCH], halo.at[dst, 0:PATCH]
    return pltpu.make_async_remote_copy(
        src_ref=a, dst_ref=b, send_sem=send, recv_sem=recv, device_id=device, device_id_type=MESH_ID
    )


def mask_copy(mask, dr, dc, send, recv, device):
    src, dst = send_slices(dr, dc)
    if dr == 0:
        a, b = mask.at[0:2, src], mask.at[0:2, dst]
    elif dr < 0:
        a, b = mask.at[0:1, src], mask.at[3:4, dst]
    else:
        a, b = mask.at[1:2, src], mask.at[2:3, dst]
    return pltpu.make_async_remote_copy(
        src_ref=a, dst_ref=b, send_sem=send, recv_sem=recv, device_id=device, device_id_type=MESH_ID
    )


NT = (((1,), (1,)), ((), ()))
TN = (((0,), (0,)), ((), ()))


def eye(n):
    return lax.broadcasted_iota(jnp.int32, (n, n), 0) == lax.broadcasted_iota(jnp.int32, (n, n), 1)


def affinity(
    row, col, feat, tissue, e_ref, scale_ref, mine_ref, diag_ref, own, halo, mask, deg,
    usend, urecv, csend, crecv, msend, mrecv, ready, meanwhile,
):

    for k in (2, 3):
        mask[k] = jnp.zeros((TC + 2, 8, 128), jnp.float32)
    for k in (0, 1):
        mask[k, 0] = jnp.zeros((8, 128), jnp.float32)
        mask[k, TC + 1] = jnp.zeros((8, 128), jnp.float32)
        t = tissue[k].astype(jnp.float32)
        t = jnp.concatenate([t, t], axis=1)
        for c in range(TC):
            mask[k, c + 1] = jnp.broadcast_to(t[c : c + 1, :], (8, 128))

    ready()

    def edges(step, fn):
        first = 1 + step * WIDTH
        for k in (0, 1):
            dr = DIRS[k][0]
            fn(
                k,
                halo_copy(
                    own, halo, dr, 0, usend.at[k, step], urecv.at[k, step],
                    device_at(row + dr, col), first, WIDTH,
                ),
            )

    def start_edges(step):
        def go(k, copy):
            @pl.when(inside(row + DIRS[k][0], col))
            def _():
                copy.start()

        edges(step, go)

    def normalise(c):
        for k in (0, 1):
            v = feat[k, c].astype(jnp.float32)
            total = jnp.sum(v * v, axis=-1, keepdims=True)
            own[c + 1, k * PATCH : (k + 1) * PATCH] = (v * lax.rsqrt(total + 1e-06)).astype(
                jnp.bfloat16
            )

    for c in range(WIDTH):
        normalise(c)

    def group(step, _):
        for i in range(WIDTH):
            normalise(step * WIDTH + i)
        start_edges(step - 1)
        return 0

    lax.fori_loop(1, STEPS, group, 0)
    start_edges(STEPS - 1)

    def side(k):
        dr, dc = DIRS[k]
        device = device_at(row + dr, col + dc)
        return halo_copy(own, halo, dr, dc, csend.at[k], crecv.at[k], device)

    def side_mask(k):
        dr, dc = DIRS[k]
        device = device_at(row + dr, col + dc)
        return mask_copy(mask, dr, dc, msend.at[k], mrecv.at[k], device)

    for k, (dr, dc) in enumerate(DIRS):

        @pl.when(inside(row + dr, col + dc))
        def _(k=k):
            side_mask(k).start()
            if k >= 2:
                side(k).start()

    lane = lax.broadcasted_iota(jnp.int32, (128, 128), 1)
    sub = lax.broadcasted_iota(jnp.int32, (128, 128), 0)
    diagonal = lane == sub
    seen = (lane < PATCH) == (sub < PATCH)

    def block(c, cc, other, upper, lower, kind):
        s = lax.dot_general(own[c], other[cc], NT, preferred_element_type=jnp.float32)
        w = jnp.exp(AFFINITY_TEMP * (s - 1.0))
        m = jnp.where(lane[0:1] < PATCH, upper[cc, 0:1], lower[cc, 0:1])
        keep = jnp.broadcast_to(m, (128, 128)) > 0.5
        if kind == 1:
            keep = keep & seen
        return jnp.where(keep, w, 0.0)

    def own_blocks(c, parts):
        total = jnp.zeros((128, 1), jnp.float32)
        for d in parts:
            w = block(c, c + d - 1, own, mask.at[0], mask.at[1], 0)
            total = total + jnp.sum(w, axis=1, keepdims=True)
            if d == 1:
                self_w = jnp.sum(jnp.where(diagonal, w, 0.0), axis=1, keepdims=True)
                diag_ref[c - 1] = jnp.broadcast_to(self_w, (128, 128))
                w = jnp.where(diagonal, 0.0, w)
            e_ref[c - 1, 0, :, d * 128 : (d + 1) * 128] = w.astype(jnp.bfloat16)
        return total

    def halo_blocks(c):
        total = jnp.zeros((128, 1), jnp.float32)
        for d in range(3):
            w = block(c, c + d - 1, halo, mask.at[2], mask.at[3], 1)
            total = total + jnp.sum(w, axis=1, keepdims=True)
            e_ref[c - 1, 1, :, d * 128 : (d + 1) * 128] = w.astype(jnp.bfloat16)
        return total

    def inner(c, _):
        deg[c] = jnp.broadcast_to(own_blocks(c, (0, 1, 2)), (128, 128))
        return 0

    meanwhile()
    lax.fori_loop(2, TC, inner, 0, unroll=2)

    for k, (dr, dc) in enumerate(DIRS):

        @pl.when(inside(row - dr, col - dc))
        def _(k=k):
            side_mask(k).wait_recv()
            if k >= 2:
                side(k).wait_recv()

    for c in (1, TC):
        deg[c] = jnp.broadcast_to(own_blocks(c, (0, 1, 2)), (128, 128))

    def finish(c):
        total = deg[c][:, 0:1] + halo_blocks(c)
        m = jnp.where(lane[0:1] < PATCH, mask[0, c, 0:1], mask[1, c, 0:1])
        mine = jnp.sum(jnp.where(diagonal, jnp.broadcast_to(m, (128, 128)), 0.0), axis=1, keepdims=True)
        scale = lax.rsqrt(1.0 + mine * total)
        self_w = diag_ref[c - 1]
        scale_ref[c - 1] = jnp.broadcast_to(scale, (128, 128))
        mine_ref[c - 1] = jnp.broadcast_to(scale * mine, (128, 128))
        diag_ref[c - 1] = 1.0 + (mine * scale * scale) * self_w

    def wait_edges(step):
        def go(k, copy):
            @pl.when(inside(row - DIRS[k][0], col))
            def _():
                copy.wait_recv()

        edges(step, go)

    wait_edges(0)
    for c in range(1, WIDTH):
        finish(c)

    def halo_group(step, _):
        wait_edges(step)
        for i in range(WIDTH):
            finish(step * WIDTH + i)
        return 0

    lax.fori_loop(1, STEPS, halo_group, 0)
    finish(TC)

    def drain(step, _):
        def go(k, copy):
            @pl.when(inside(row + DIRS[k][0], col))
            def _():
                copy.wait_send()

        edges(step, go)
        return 0

    lax.fori_loop(0, STEPS, drain, 0)
    for k, (dr, dc) in enumerate(DIRS):

        @pl.when(inside(row + dr, col + dc))
        def _(k=k):
            side_mask(k).wait_send()
            if k >= 2:
                side(k).wait_send()


def stage_peers(pos):
    z = pos[3] * 2 + pos[0]
    core = (pos[4], [(pos[0], pos[1], pos[2], pos[3], 1 - pos[4])])
    x = (pos[1], [(pos[0], (pos[1] + d) % 4, pos[2], pos[3], pos[4]) for d in (1, 2, 3)])
    y = (pos[2], [(pos[0], pos[1], (pos[2] + d) % 4, pos[3], pos[4]) for d in (1, 2, 3)])
    along = [(z + d) % 4 for d in (1, 2, 3)]
    zz = (z, [(q % 2, pos[1], pos[2], q // 2, pos[4]) for q in along])
    return [core, y, zz, x]


def inverse_factor(gram):
    n = RANK
    m = jnp.concatenate([gram, jnp.where(eye(n), 1.0, 0.0)], axis=1)
    sub = lax.broadcasted_iota(jnp.int32, (n, 2 * n), 0)
    lane = lax.broadcasted_iota(jnp.int32, (n, 2 * n), 1)
    for k in range(n - 1):
        column = jnp.broadcast_to(m[:, k : k + 1], (n, 2 * n))
        pivot = column[k : k + 1, :]
        line = m[k : k + 1, :] / pivot
        m = m - jnp.where(sub > k, column, 0.0) * line
    d = jnp.sum(jnp.where(lane == sub, m, 0.0), axis=1, keepdims=True)
    return m[:, n:] * lax.rsqrt(d)


def pair_of(v, low):
    hi = v.astype(jnp.bfloat16)
    lo = (v - hi.astype(jnp.float32)).astype(jnp.bfloat16)
    return jnp.where(low, hi, lo)


def kernel(
    feat, tissue, probe, out_ref,
    ufeat, hfeat, mask, deg, e_ref, scale_ref, mine_ref, diag_ref,
    own, halo, acc, y, pair, total, gsum,
    usend, urecv, csend, crecv, msend, mrecv, psend, precv, gsend, grecv,
):
    pos = position()
    row, col = row_col(pos)
    stages = stage_peers(pos)
    low = lax.broadcasted_iota(jnp.int32, (128, 128), 1) < RANK
    zero = jnp.zeros((128, 128), jnp.bfloat16)

    def clear(i, _):
        own[i, 0] = zero
        own[i, TC + 1] = zero

        def one(c, _):
            halo[i, c] = zero
            return 0

        lax.fori_loop(0, TC + 2, one, 0, unroll=6)
        return 0

    lax.fori_loop(0, ITERS, clear, 0)

    def ready():
        barrier(row, col, [p for _, peers in stages for p in peers])

    def meanwhile():
        def load(c, _):
            for k in (0, 1):
                v = probe[k, c]
                y[c, k * PATCH : (k + 1) * PATCH] = jnp.concatenate([v, v], axis=1)
            return 0

        lax.fori_loop(0, TC, load, 0, unroll=4)

    affinity(
        row, col, feat, tissue, e_ref, scale_ref, mine_ref, diag_ref, ufeat, hfeat, mask, deg,
        usend, urecv, csend, crecv, msend, mrecv, ready, meanwhile,
    )

    def panel(t, k):
        dr, dc = DIRS[k]
        return halo_copy(
            own.at[t], halo.at[t], dr, dc, psend.at[t, k], precv.at[t, k],
            device_at(row + dr, col + dc),
        )

    def each_target(fn):
        for k, (dr, dc) in enumerate(DIRS):

            @pl.when(inside(row + dr, col + dc))
            def _(k=k):
                fn(k)

    def each_source(fn):
        for k, (dr, dc) in enumerate(DIRS):

            @pl.when(inside(row - dr, col - dc))
            def _(k=k):
                fn(k)

    def own_part(t, first, stop):
        def go(c, _):
            b = own[t, pl.ds(c, 3)].reshape(384, 128)
            acc[c] = jnp.dot(e_ref[c, 0], b, preferred_element_type=jnp.float32)
            return 0

        lax.fori_loop(first, stop, go, 0, unroll=stop - first)

    def product(t, c):
        b = halo[t, pl.ds(c, 3)].reshape(384, 128)
        v = acc[c] + jnp.dot(e_ref[c, 1], b, preferred_element_type=jnp.float32)
        v = v + pltpu.roll(v, RANK, 1)
        return y[c] * diag_ref[c] + mine_ref[c] * v

    def start_stage(t, s, packed):
        place, peers = stages[s]
        gsum[t, s, place] = packed
        for d, there in enumerate(peers):
            pltpu.make_async_remote_copy(
                src_ref=gsum.at[t, s, place],
                dst_ref=gsum.at[t, s, place],
                send_sem=gsend.at[t, s, d],
                recv_sem=grecv.at[t, s, d],
                device_id=there,
                device_id_type=MESH_ID,
            ).start()

    def end_stage(t, s):
        place, peers = stages[s]
        n = len(peers) + 1
        for d, there in enumerate(peers):
            pltpu.make_async_remote_copy(
                src_ref=gsum.at[t, s, place],
                dst_ref=gsum.at[t, s, (place + n - 1 - d) % n],
                send_sem=gsend.at[t, s, d],
                recv_sem=grecv.at[t, s, d],
                device_id=there,
                device_id_type=MESH_ID,
            ).wait_recv()
        packed = gsum[t, s, 0]
        for i in range(1, n):
            packed = packed + gsum[t, s, i]
        return packed

    def new_rows(t, c, v):
        p = pair_of(v, low)
        total[...] += lax.dot_general(p, p, TN, preferred_element_type=jnp.float32)
        if t < ITERS - 1:
            y[c] = v
            own[t + 1, c + 1] = pair_of(v * scale_ref[c], low)
        else:
            pair[c] = p

    def solver(packed):
        gram = jnp.concatenate([packed[:, :64], packed[:, 64:]], axis=0)
        inv = inverse_factor(gram)
        hi = inv.astype(jnp.bfloat16)
        lo = (inv - hi.astype(jnp.float32)).astype(jnp.bfloat16)
        both = jnp.concatenate([hi, hi, lo, lo], axis=1)
        both = jnp.concatenate([both, both], axis=0)

        def solve(p):
            p = jnp.concatenate([p, p], axis=1)
            return lax.dot_general(p, both, NT, preferred_element_type=jnp.float32)

        return solve

    def first(c, _):
        own[0, c + 1] = pair_of(y[c] * scale_ref[c], low)
        return 0

    lax.fori_loop(0, TC, first, 0, unroll=4)
    each_target(lambda k: panel(0, k).start())
    own_part(0, 1, TC - 1)
    each_source(lambda k: panel(0, k).wait_recv())
    own_part(0, 0, 1)
    own_part(0, TC - 1, TC)
    total[...] = jnp.zeros((128, 128), jnp.float32)

    def rows0(c, _):
        new_rows(0, c, product(0, c))
        return 0

    lax.fori_loop(0, TC, rows0, 0, unroll=8)

    solve = None
    for t in range(ITERS):
        g = total[...]
        g = g[:, :64] + g[:, 64:]
        g = g[:64] + g[64:]
        packed = jnp.concatenate([g[:32], g[32:]], axis=1)
        more = t < ITERS - 1
        start_stage(t, 0, packed)
        if more:
            each_target(lambda k: panel(t + 1, k).start())
            own_part(t + 1, 1, 5)
        start_stage(t, 1, end_stage(t, 0))
        if more:
            own_part(t + 1, 5, 10)
        start_stage(t, 2, end_stage(t, 1))
        if more:
            own_part(t + 1, 10, TC - 1)
        start_stage(t, 3, end_stage(t, 2))
        if more:
            each_source(lambda k: panel(t + 1, k).wait_recv())
            own_part(t + 1, 0, 1)
            own_part(t + 1, TC - 1, TC)

            def apply(c, _):
                pair[c] = pair_of(product(t + 1, c), low)
                return 0

            lax.fori_loop(0, TC, apply, 0, unroll=8)
        solve = solver(end_stage(t, 3))
        if more:
            total[...] = jnp.zeros((128, 128), jnp.float32)

            def rows(c, _):
                new_rows(t + 1, c, solve(pair[c]))
                return 0

            lax.fori_loop(0, TC, rows, 0, unroll=8)

    factor = math.sqrt(float(NROW * 2 * NCOL * TC * PATCH))

    def last(c, _):
        v = factor * solve(pair[c])
        for k in (0, 1):
            out_ref[k, c] = v[k * PATCH : (k + 1) * PATCH, :RANK]
        return 0

    lax.fori_loop(0, TC, last, 0, unroll=4)

    for t in range(ITERS):
        each_target(lambda k: panel(t, k).wait_send())
        for s, (place, peers) in enumerate(stages):
            for d, there in enumerate(peers):
                pltpu.make_async_remote_copy(
                    src_ref=gsum.at[t, s, place],
                    dst_ref=gsum.at[t, s, place],
                    send_sem=gsend.at[t, s, d],
                    recv_sem=grecv.at[t, s, d],
                    device_id=there,
                    device_id_type=MESH_ID,
                ).wait_send()


VM = pl.BlockSpec(memory_space=pltpu.VMEM)
DMA = pltpu.SemaphoreType.DMA
LIMIT = 60 * 2**20


def local(features, tissue, probe):
    width = features.shape[-1]
    full = (TC, 128, 128)
    wide = (TC + 2, 128, width)
    out = pl.pallas_call(
        kernel,
        out_shape=jax.ShapeDtypeStruct((2, TC, PATCH, RANK), jnp.float32),
        in_specs=[VM] * 3,
        out_specs=VM,
        scratch_shapes=[
            pltpu.VMEM(wide, jnp.bfloat16),
            pltpu.VMEM(wide, jnp.bfloat16),
            pltpu.VMEM((4, TC + 2, 8, 128), jnp.float32),
            pltpu.VMEM((TC + 1, 128, 128), jnp.float32),
            pltpu.VMEM((TC, 2, 128, 384), jnp.bfloat16),
            pltpu.VMEM(full, jnp.float32),
            pltpu.VMEM(full, jnp.float32),
            pltpu.VMEM(full, jnp.float32),
            pltpu.VMEM((ITERS, TC + 2, 128, 128), jnp.bfloat16),
            pltpu.VMEM((ITERS, TC + 2, 128, 128), jnp.bfloat16),
            pltpu.VMEM(full, jnp.float32),
            pltpu.VMEM(full, jnp.float32),
            pltpu.VMEM(full, jnp.bfloat16),
            pltpu.VMEM((128, 128), jnp.float32),
            pltpu.VMEM((ITERS, 4, 4, 32, 128), jnp.float32),
            DMA((2, STEPS)), DMA((2, STEPS)), DMA((8,)), DMA((8,)), DMA((8,)), DMA((8,)),
            DMA((ITERS, 8)), DMA((ITERS, 8)), DMA((ITERS, 4, 3)), DMA((ITERS, 4, 3)),
        ],
        compiler_params=pltpu.CompilerParams(
            collective_id=0, has_side_effects=True, vmem_limit_bytes=LIMIT
        ),
        name="range_finder",
    )(features, tissue, probe.reshape(2, TC, PATCH, RANK))
    return out.reshape(2, TC, PATCH * RANK)


def solution(mesh):
    torus = Mesh(mesh.devices.reshape(2, 4, 4, 2, 2), AXES)
    return jax.shard_map(
        local,
        mesh=torus,
        in_specs=(P(ROW, COL, None, None), P(ROW, COL, None), P(ROW, COL, None)),
        out_specs=P(ROW, COL, None),
        check_vma=False,
    )
```

```python
import functools
import math

import jax
import jax.numpy as jnp
from jax import lax
from jax.experimental import pallas as pl
from jax.experimental.pallas import tpu as pltpu
from jax.sharding import Mesh
from jax.sharding import PartitionSpec as P

RANK = 64
ITERS = 3
PATCH = 64
AXES = ("row_0", "row_1", "col_0", "col_1", "col_2")
ROW = ("row_0", "row_1")
COL = ("col_0", "col_1", "col_2")
NROW, NCOL = 8, 16
TC = 16
MESH_ID = pl.DeviceIdType.MESH
AFFINITY_TEMP = 4.0

DIRS = ((-1, 0), (1, 0), (0, -1), (0, 1), (-1, -1), (-1, 1), (1, -1), (1, 1))


def position():
    return tuple(lax.axis_index(a) for a in AXES)


def row_col(pos):
    return pos[0] * 4 + pos[1], pos[2] * 4 + pos[3] * 2 + pos[4]


def device_at(row, col):
    row = jnp.clip(row, 0, NROW - 1)
    col = jnp.clip(col, 0, NCOL - 1)
    return (row // 4, row % 4, col // 4, (col // 2) % 2, col % 2)


def inside(row, col):
    return (row >= 0) & (row < NROW) & (col >= 0) & (col < NCOL)


def barrier(row, col, others):
    sem = pltpu.get_barrier_semaphore()
    for dr, dc in DIRS:

        @pl.when(inside(row + dr, col + dc))
        def _(dr=dr, dc=dc):
            pl.semaphore_signal(
                sem, inc=1, device_id=device_at(row + dr, col + dc), device_id_type=MESH_ID
            )

    for other in others:
        pl.semaphore_signal(sem, inc=1, device_id=other, device_id_type=MESH_ID)
    near = sum(inside(row + dr, col + dc).astype(jnp.int32) for dr, dc in DIRS)
    pl.semaphore_wait(sem, near + len(others))


def send_slices(dr, dc, first=1, count=TC):
    if dc == 0:
        src, dst = pl.ds(first, count), pl.ds(first, count)
    elif dc < 0:
        src, dst = pl.ds(1, 1), pl.ds(TC + 1, 1)
    else:
        src, dst = pl.ds(TC, 1), pl.ds(0, 1)
    return src, dst


def halo_copy(own, halo, dr, dc, send, recv, device, first=1, count=TC):
    src, dst = send_slices(dr, dc, first, count)
    if dr == 0:
        a, b = own.at[src], own.at[dst]
    elif dr < 0:
        a, b = own.at[src, 0:PATCH], halo.at[dst, PATCH : 2 * PATCH]
    else:
        a, b = own.at[src, PATCH : 2 * PATCH], halo.at[dst, 0:PATCH]
    return pltpu.make_async_remote_copy(
        src_ref=a, dst_ref=b, send_sem=send, recv_sem=recv, device_id=device, device_id_type=MESH_ID
    )


def mask_copy(mask, dr, dc, send, recv, device):
    src, dst = send_slices(dr, dc)
    if dr == 0:
        a, b = mask.at[0:2, src], mask.at[0:2, dst]
    elif dr < 0:
        a, b = mask.at[0:1, src], mask.at[3:4, dst]
    else:
        a, b = mask.at[1:2, src], mask.at[2:3, dst]
    return pltpu.make_async_remote_copy(
        src_ref=a, dst_ref=b, send_sem=send, recv_sem=recv, device_id=device, device_id_type=MESH_ID
    )


NT = (((1,), (1,)), ((), ()))
TN = (((0,), (0,)), ((), ()))


def eye(n):
    return lax.broadcasted_iota(jnp.int32, (n, n), 0) == lax.broadcasted_iota(jnp.int32, (n, n), 1)


def affinity(
    row, col, feat, tissue, e_ref, eh_ref, scale_ref, mine_ref, diag_ref, own, halo, mask, deg, served,
    fsend, frecv, csend, crecv, msend, mrecv, rsend, rrecv, ready, meanwhile,
):
    for k in (2, 3):
        mask[k] = jnp.zeros((TC + 2, 8, 128), jnp.float32)
    for k in (0, 1):
        mask[k, 0] = jnp.zeros((8, 128), jnp.float32)
        mask[k, TC + 1] = jnp.zeros((8, 128), jnp.float32)
        t = tissue[k].astype(jnp.float32)
        t = jnp.concatenate([t, t], axis=1)
        for c in range(TC):
            mask[k, c + 1] = jnp.broadcast_to(t[c : c + 1, :], (8, 128))

    def nothing(c, _):
        for side in (0, 1):
            eh_ref[side, c] = jnp.zeros((PATCH, 256), jnp.bfloat16)
        return 0

    lax.fori_loop(0, TC, nothing, 0, unroll=4)
    ready()

    there = [inside(row - 1, col), inside(row + 1, col)]
    device = [device_at(row - 1, col), device_at(row + 1, col)]

    def tile_copy(side, c):
        return pltpu.make_async_remote_copy(
            src_ref=own.at[c, side * PATCH : (side + 1) * PATCH],
            dst_ref=halo.at[c, (1 - side) * PATCH : (2 - side) * PATCH],
            send_sem=fsend.at[side, c],
            recv_sem=frecv.at[1 - side, c],
            device_id=device[side],
            device_id_type=MESH_ID,
        )

    def tile_arrival(side, c):
        return pltpu.make_async_remote_copy(
            src_ref=own.at[c, side * PATCH : (side + 1) * PATCH],
            dst_ref=halo.at[c, side * PATCH : (side + 1) * PATCH],
            send_sem=fsend.at[side, c],
            recv_sem=frecv.at[side, c],
            device_id=device[side],
            device_id_type=MESH_ID,
        )

    def weights_copy(side, c):
        return pltpu.make_async_remote_copy(
            src_ref=served.at[side, c - 1],
            dst_ref=eh_ref.at[1 - side, c - 1],
            send_sem=rsend.at[side, c],
            recv_sem=rrecv.at[1 - side, c],
            device_id=device[side],
            device_id_type=MESH_ID,
        )

    def weights_arrival(side, c):
        return pltpu.make_async_remote_copy(
            src_ref=served.at[side, c - 1],
            dst_ref=eh_ref.at[side, c - 1],
            send_sem=rsend.at[side, c],
            recv_sem=rrecv.at[side, c],
            device_id=device[side],
            device_id_type=MESH_ID,
        )

    def on(side, fn):
        @pl.when(there[side])
        def _():
            fn()

    def normalise(c):
        for k in (0, 1):
            v = feat[k, c - 1].astype(jnp.float32)
            total = jnp.sum(v * v, axis=-1, keepdims=True)
            own[c, k * PATCH : (k + 1) * PATCH] = (v * lax.rsqrt(total + 1e-06)).astype(
                jnp.bfloat16
            )

    def side_copy(k):
        dr, dc = DIRS[k]
        return halo_copy(own, halo, dr, dc, csend.at[k], crecv.at[k], device_at(row, col + dc))

    def side_mask(k):
        dr, dc = DIRS[k]
        return mask_copy(mask, dr, dc, msend.at[k], mrecv.at[k], device_at(row + dr, col + dc))

    for k in range(4):
        dr, dc = DIRS[k]

        @pl.when(inside(row + dr, col + dc))
        def _(k=k):
            side_mask(k).start()

    half = TC // 2
    normalise(1)
    normalise(TC)
    normalise(2)
    normalise(TC - 1)
    for side in (0, 1):
        on(side, lambda side=side: (tile_copy(side, 1).start(), tile_copy(side, TC).start()))
    for k in (2, 3):

        @pl.when(inside(row, col + DIRS[k][1]))
        def _(k=k):
            side_copy(k).start()

    def group(g, _):
        normalise(g + 1)
        normalise(TC - g)
        on(0, lambda: tile_copy(0, TC + 1 - g).start())
        on(1, lambda: tile_copy(1, g).start())
        return 0

    lax.fori_loop(2, half, group, 0)
    on(0, lambda: tile_copy(0, half + 1).start())
    on(1, lambda: (tile_copy(1, half).start(), tile_copy(1, half + 1).start()))

    lane = lax.broadcasted_iota(jnp.int32, (128, 128), 1)
    sub = lax.broadcasted_iota(jnp.int32, (128, 128), 0)
    diagonal = lane == sub
    first = lane[0:1] < PATCH

    def block(c, cc):
        s = lax.dot_general(own[c], own[cc], NT, preferred_element_type=jnp.float32)
        w = jnp.exp(AFFINITY_TEMP * (s - 1.0))
        m = jnp.where(first, mask[0, cc, 0:1], mask[1, cc, 0:1])
        return jnp.where(jnp.broadcast_to(m, (128, 128)) > 0.5, w, 0.0)

    def own_blocks(c):
        total = jnp.zeros((128, 1), jnp.float32)
        for d in range(3):
            w = block(c, c + d - 1)
            total = total + jnp.sum(w, axis=1, keepdims=True)
            if d == 1:
                self_w = jnp.sum(jnp.where(diagonal, w, 0.0), axis=1, keepdims=True)
                diag_ref[c - 1] = jnp.broadcast_to(self_w, (128, 128))
                w = jnp.where(diagonal, 0.0, w)
            e_ref[c - 1, :, d * 128 : (d + 1) * 128] = w.astype(jnp.bfloat16)
        deg[c] = jnp.broadcast_to(total, (128, 128))

    meanwhile()

    for k in range(4):
        dr, dc = DIRS[k]

        @pl.when(inside(row - dr, col - dc))
        def _(k=k):
            side_mask(k).wait_recv()
            if k >= 2:
                side_copy(k).wait_recv()

    def rows_of(left, right, right_mask, c):
        s = lax.dot_general(left, right, NT, preferred_element_type=jnp.float32)
        w = jnp.exp(AFFINITY_TEMP * (s - 1.0))
        m0 = jnp.where(first, mask[right_mask, c - 1, 0:1], mask[right_mask, c, 0:1])
        m1 = mask[right_mask, c + 1, 0:1]
        w0 = jnp.where(jnp.broadcast_to(m0, (PATCH, 128)) > 0.5, w[:, :128], 0.0)
        w1 = jnp.where(jnp.broadcast_to(m1[:, :PATCH], (PATCH, PATCH)) > 0.5, w[:, 128:], 0.0)
        w1 = jnp.concatenate([w1, jnp.zeros((PATCH, PATCH), jnp.float32)], axis=1)
        return jnp.concatenate([w0, w1], axis=1).astype(jnp.bfloat16)

    def near(ref, side, c):
        return ref[pl.ds(c - 1, 3), side * PATCH : (side + 1) * PATCH].reshape(3 * PATCH, -1)

    def serve(side, c):
        tile_arrival(side, c).wait_recv()
        left = halo[c, side * PATCH : (side + 1) * PATCH]
        served[side, c - 1] = rows_of(left, near(own, side, c), side, c)
        weights_copy(side, c).start()

    def at_home(side, c):
        left = own[c, side * PATCH : (side + 1) * PATCH]
        eh_ref[side, c - 1] = rows_of(left, near(halo, side, c), 2 + side, c)

    def inner(c, _):
        own_blocks(c)
        return 0

    lax.fori_loop(1, 4, inner, 0)
    for c in (1, TC):
        for side in (0, 1):
            on(side, lambda side=side, c=c: serve(side, c))
    lax.fori_loop(4, 6, inner, 0)
    on(0, lambda: serve(0, 2))
    on(1, lambda: serve(1, TC - 1))

    def arrive(g, _):
        on(0, lambda: (serve(0, g + 1), at_home(0, g)))
        on(1, lambda: (serve(1, TC - g), at_home(1, TC + 1 - g)))

        @pl.when(g < 7)
        def _():
            own_blocks(2 * g + 2)
            own_blocks(2 * g + 3)

        @pl.when(g == 7)
        def _():
            own_blocks(TC)

        return 0

    lax.fori_loop(2, half, arrive, 0)
    on(0, lambda: (serve(0, half + 1), at_home(0, half)))

    def finish(c):
        eh = jnp.concatenate([eh_ref[0, c - 1], eh_ref[1, c - 1]], axis=0).astype(jnp.float32)
        total = deg[c][:, 0:1] + jnp.sum(eh, axis=1, keepdims=True)
        m = jnp.where(first, mask[0, c, 0:1], mask[1, c, 0:1])
        mine = jnp.sum(jnp.where(diagonal, jnp.broadcast_to(m, (128, 128)), 0.0), axis=1, keepdims=True)
        scale = lax.rsqrt(1.0 + mine * total)
        self_w = diag_ref[c - 1]
        scale_ref[c - 1] = jnp.broadcast_to(scale, (128, 128))
        mine_ref[c - 1] = jnp.broadcast_to(scale * mine, (128, 128))
        diag_ref[c - 1] = 1.0 + (mine * scale * scale) * self_w

    def back(side, columns):
        for c in columns:
            weights_arrival(side, c).wait_recv()

    up = [1] + list(range(half + 1, TC + 1))
    down = list(range(1, half + 2)) + [TC]
    on(0, lambda: back(0, up))
    on(1, lambda: back(1, down))

    def finish_one(c, _):
        finish(c)
        return 0

    lax.fori_loop(1, TC + 1, finish_one, 0, unroll=4)

    def sent():
        for side, mine, theirs in ((0, up, down), (1, down, up)):

            def go(side=side, mine=mine, theirs=theirs):
                for c in mine:
                    tile_copy(side, c).wait_send()
                for c in theirs:
                    weights_copy(side, c).wait_send()

            on(side, go)
        for k in range(4):
            dr, dc = DIRS[k]

            @pl.when(inside(row + dr, col + dc))
            def _(k=k):
                side_mask(k).wait_send()
                if k >= 2:
                    side_copy(k).wait_send()

    return sent


def stage_peers(pos):
    z = pos[3] * 2 + pos[0]
    core = (pos[4], [(pos[0], pos[1], pos[2], pos[3], 1 - pos[4])])
    x = (pos[1], [(pos[0], (pos[1] + d) % 4, pos[2], pos[3], pos[4]) for d in (1, 2, 3)])
    y = (pos[2], [(pos[0], pos[1], (pos[2] + d) % 4, pos[3], pos[4]) for d in (1, 2, 3)])
    along = [(z + d) % 4 for d in (1, 2, 3)]
    zz = (z, [(q % 2, pos[1], pos[2], q // 2, pos[4]) for q in along])
    return [core, y, zz, x]


def inverse_factor(gram):
    n = RANK
    m = jnp.concatenate([gram, jnp.where(eye(n), 1.0, 0.0)], axis=1)
    sub = lax.broadcasted_iota(jnp.int32, (n, 2 * n), 0)
    lane = lax.broadcasted_iota(jnp.int32, (n, 2 * n), 1)
    for k in range(n - 1):
        column = jnp.broadcast_to(m[:, k : k + 1], (n, 2 * n))
        pivot = column[k : k + 1, :]
        line = m[k : k + 1, :] / pivot
        m = m - jnp.where(sub > k, column, 0.0) * line
    d = jnp.sum(jnp.where(lane == sub, m, 0.0), axis=1, keepdims=True)
    return m[:, n:] * lax.rsqrt(d)


def pair_of(v, low):
    hi = v.astype(jnp.bfloat16)
    lo = (v - hi.astype(jnp.float32)).astype(jnp.bfloat16)
    return jnp.where(low, hi, lo)


def kernel(
    feat, tissue, probe, out_ref,
    ufeat, hfeat, mask, deg, served, e_ref, eh_ref, scale_ref, mine_ref, diag_ref,
    own, halo, acc, y, pair, total, gsum,
    fsend, frecv, csend, crecv, msend, mrecv, rsend, rrecv, psend, precv, gsend, grecv,
):
    pos = position()
    row, col = row_col(pos)
    stages = stage_peers(pos)
    low = lax.broadcasted_iota(jnp.int32, (128, 128), 1) < RANK
    zero = jnp.zeros((128, 128), jnp.bfloat16)

    def clear(i, _):
        own[i, 0] = zero
        own[i, TC + 1] = zero

        def one(c, _):
            for side in (0, 1):
                halo[i, side, c] = zero[:PATCH]
            return 0

        lax.fori_loop(0, TC + 3, one, 0)
        return 0

    lax.fori_loop(0, ITERS, clear, 0)

    def ready():
        barrier(row, col, [p for _, peers in stages for p in peers])

    def meanwhile():
        def load(c, _):
            for k in (0, 1):
                v = probe[k, c]
                y[c, k * PATCH : (k + 1) * PATCH] = jnp.concatenate([v, v], axis=1)
            return 0

        lax.fori_loop(0, TC, load, 0, unroll=4)

    sent = affinity(
        row, col, feat, tissue, e_ref, eh_ref, scale_ref, mine_ref, diag_ref, ufeat, hfeat, mask,
        deg, served, fsend, frecv, csend, crecv, msend, mrecv, rsend, rrecv, ready, meanwhile,
    )

    def panel(t, k):
        dr, dc = DIRS[k]
        src, dst = send_slices(dr, dc)
        if dr == 0:
            a, b = own.at[t, src], own.at[t, dst]
        elif dr < 0:
            a, b = own.at[t, src, 0:PATCH], halo.at[t, 1, dst]
        else:
            a, b = own.at[t, src, PATCH : 2 * PATCH], halo.at[t, 0, dst]
        return pltpu.make_async_remote_copy(
            src_ref=a, dst_ref=b, send_sem=psend.at[t, k], recv_sem=precv.at[t, k],
            device_id=device_at(row + dr, col + dc), device_id_type=MESH_ID,
        )

    def each_target(fn):
        for k, (dr, dc) in enumerate(DIRS):

            @pl.when(inside(row + dr, col + dc))
            def _(k=k):
                fn(k)

    def each_source(fn):
        for k, (dr, dc) in enumerate(DIRS):

            @pl.when(inside(row - dr, col - dc))
            def _(k=k):
                fn(k)

    def own_part(t, first, stop):
        def go(c, _):
            b = own[t, pl.ds(c, 3)].reshape(384, 128)
            acc[c] = jnp.dot(e_ref[c], b, preferred_element_type=jnp.float32)
            return 0

        lax.fori_loop(first, stop, go, 0, unroll=stop - first)

    def product(t, c):
        v = [
            jnp.dot(
                eh_ref[side, c],
                halo[t, side, pl.ds(c, 4)].reshape(256, 128),
                preferred_element_type=jnp.float32,
            )
            for side in (0, 1)
        ]
        v = acc[c] + jnp.concatenate(v, axis=0)
        v = v + pltpu.roll(v, RANK, 1)
        return y[c] * diag_ref[c] + mine_ref[c] * v

    def start_stage(t, s, packed):
        place, peers = stages[s]
        gsum[t, s, place] = packed
        for d, there in enumerate(peers):
            pltpu.make_async_remote_copy(
                src_ref=gsum.at[t, s, place],
                dst_ref=gsum.at[t, s, place],
                send_sem=gsend.at[t, s, d],
                recv_sem=grecv.at[t, s, d],
                device_id=there,
                device_id_type=MESH_ID,
            ).start()

    def end_stage(t, s):
        place, peers = stages[s]
        n = len(peers) + 1
        for d, there in enumerate(peers):
            pltpu.make_async_remote_copy(
                src_ref=gsum.at[t, s, place],
                dst_ref=gsum.at[t, s, (place + n - 1 - d) % n],
                send_sem=gsend.at[t, s, d],
                recv_sem=grecv.at[t, s, d],
                device_id=there,
                device_id_type=MESH_ID,
            ).wait_recv()
        packed = gsum[t, s, 0]
        for i in range(1, n):
            packed = packed + gsum[t, s, i]
        return packed

    def new_rows(t, c, v):
        p = pair_of(v, low)
        total[...] += lax.dot_general(p, p, TN, preferred_element_type=jnp.float32)
        if t < ITERS - 1:
            y[c] = v
            own[t + 1, c + 1] = pair_of(v * scale_ref[c], low)
        else:
            pair[c] = p

    def solver(packed):
        gram = jnp.concatenate([packed[:, :64], packed[:, 64:]], axis=0)
        inv = inverse_factor(gram)
        hi = inv.astype(jnp.bfloat16)
        lo = (inv - hi.astype(jnp.float32)).astype(jnp.bfloat16)
        both = jnp.concatenate([hi, hi, lo, lo], axis=1)
        both = jnp.concatenate([both, both], axis=0)

        def solve(p):
            p = jnp.concatenate([p, p], axis=1)
            return lax.dot_general(p, both, NT, preferred_element_type=jnp.float32)

        return solve

    def first(c, _):
        own[0, c + 1] = pair_of(y[c] * scale_ref[c], low)
        return 0

    lax.fori_loop(0, TC, first, 0, unroll=4)
    each_target(lambda k: panel(0, k).start())
    own_part(0, 1, TC - 1)
    each_source(lambda k: panel(0, k).wait_recv())
    own_part(0, 0, 1)
    own_part(0, TC - 1, TC)
    total[...] = jnp.zeros((128, 128), jnp.float32)

    def rows0(c, _):
        new_rows(0, c, product(0, c))
        return 0

    lax.fori_loop(0, TC, rows0, 0, unroll=8)

    solve = None
    for t in range(ITERS):
        g = total[...]
        g = g[:, :64] + g[:, 64:]
        g = g[:64] + g[64:]
        packed = jnp.concatenate([g[:32], g[32:]], axis=1)
        more = t < ITERS - 1
        start_stage(t, 0, packed)
        if more:
            each_target(lambda k: panel(t + 1, k).start())
            own_part(t + 1, 1, 5)
        start_stage(t, 1, end_stage(t, 0))
        if more:
            own_part(t + 1, 5, 10)
        start_stage(t, 2, end_stage(t, 1))
        if more:
            own_part(t + 1, 10, TC - 1)
        start_stage(t, 3, end_stage(t, 2))
        if more:
            each_source(lambda k: panel(t + 1, k).wait_recv())
            own_part(t + 1, 0, 1)
            own_part(t + 1, TC - 1, TC)

            def apply(c, _):
                pair[c] = pair_of(product(t + 1, c), low)
                return 0

            lax.fori_loop(0, TC, apply, 0, unroll=8)
        solve = solver(end_stage(t, 3))
        if more:
            total[...] = jnp.zeros((128, 128), jnp.float32)

            def rows(c, _):
                new_rows(t + 1, c, solve(pair[c]))
                return 0

            lax.fori_loop(0, TC, rows, 0, unroll=8)

    factor = math.sqrt(float(NROW * 2 * NCOL * TC * PATCH))

    def last(c, _):
        v = factor * solve(pair[c])
        for k in (0, 1):
            out_ref[k, c] = v[k * PATCH : (k + 1) * PATCH, :RANK]
        return 0

    lax.fori_loop(0, TC, last, 0, unroll=4)

    sent()
    for t in range(ITERS):
        each_target(lambda k: panel(t, k).wait_send())
        for s, (place, peers) in enumerate(stages):
            for d, there in enumerate(peers):
                pltpu.make_async_remote_copy(
                    src_ref=gsum.at[t, s, place],
                    dst_ref=gsum.at[t, s, place],
                    send_sem=gsend.at[t, s, d],
                    recv_sem=grecv.at[t, s, d],
                    device_id=there,
                    device_id_type=MESH_ID,
                ).wait_send()


VM = pl.BlockSpec(memory_space=pltpu.VMEM)
DMA = pltpu.SemaphoreType.DMA
LIMIT = 60 * 2**20


def local(features, tissue, probe):
    width = features.shape[-1]
    full = (TC, 128, 128)
    wide = (TC + 2, 128, width)
    out = pl.pallas_call(
        kernel,
        out_shape=jax.ShapeDtypeStruct((2, TC, PATCH, RANK), jnp.float32),
        in_specs=[VM] * 3,
        out_specs=VM,
        scratch_shapes=[
            pltpu.VMEM(wide, jnp.bfloat16),
            pltpu.VMEM(wide, jnp.bfloat16),
            pltpu.VMEM((4, TC + 2, 8, 128), jnp.float32),
            pltpu.VMEM((TC + 1, 128, 128), jnp.float32),
            pltpu.VMEM((2, TC, PATCH, 256), jnp.bfloat16),
            pltpu.VMEM((TC, 128, 384), jnp.bfloat16),
            pltpu.VMEM((2, TC, PATCH, 256), jnp.bfloat16),
            pltpu.VMEM(full, jnp.float32),
            pltpu.VMEM(full, jnp.float32),
            pltpu.VMEM(full, jnp.float32),
            pltpu.VMEM((ITERS, TC + 2, 128, 128), jnp.bfloat16),
            pltpu.VMEM((ITERS, 2, TC + 3, PATCH, 128), jnp.bfloat16),
            pltpu.VMEM(full, jnp.float32),
            pltpu.VMEM(full, jnp.float32),
            pltpu.VMEM(full, jnp.bfloat16),
            pltpu.VMEM((128, 128), jnp.float32),
            pltpu.VMEM((ITERS, 4, 4, 32, 128), jnp.float32),
            DMA((2, TC + 1)), DMA((2, TC + 1)), DMA((4,)), DMA((4,)), DMA((4,)), DMA((4,)),
            DMA((2, TC + 1)), DMA((2, TC + 1)),
            DMA((ITERS, 8)), DMA((ITERS, 8)), DMA((ITERS, 4, 3)), DMA((ITERS, 4, 3)),
        ],
        compiler_params=pltpu.CompilerParams(
            collective_id=0, has_side_effects=True, vmem_limit_bytes=LIMIT
        ),
        name="range_finder",
    )(features, tissue, probe.reshape(2, TC, PATCH, RANK))
    return out.reshape(2, TC, PATCH * RANK)


def solution(mesh):
    torus = Mesh(mesh.devices.reshape(2, 4, 4, 2, 2), AXES)
    return jax.shard_map(
        local,
        mesh=torus,
        in_specs=(P(ROW, COL, None, None), P(ROW, COL, None), P(ROW, COL, None)),
        out_specs=P(ROW, COL, None),
        check_vma=False,
    )
```

```python
import functools
import math

import jax
import jax.numpy as jnp
from jax import lax
from jax.experimental import pallas as pl
from jax.experimental.pallas import tpu as pltpu
from jax.sharding import Mesh
from jax.sharding import PartitionSpec as P

RANK = 64
ITERS = 3
PATCH = 64
AXES = ("row_0", "row_1", "col_0", "col_1", "col_2")
ROW = ("row_0", "row_1")
COL = ("col_0", "col_1", "col_2")
NROW, NCOL = 8, 16
TC = 16
MESH_ID = pl.DeviceIdType.MESH
AFFINITY_TEMP = 4.0
LATE = 6

DIRS = ((-1, 0), (1, 0), (0, -1), (0, 1), (-1, -1), (-1, 1), (1, -1), (1, 1))


def position():
    return tuple(lax.axis_index(a) for a in AXES)


def row_col(pos):
    return pos[0] * 4 + pos[1], pos[2] * 4 + pos[3] * 2 + pos[4]


def device_at(row, col):
    row = jnp.clip(row, 0, NROW - 1)
    col = jnp.clip(col, 0, NCOL - 1)
    return (row // 4, row % 4, col // 4, (col // 2) % 2, col % 2)


def inside(row, col):
    return (row >= 0) & (row < NROW) & (col >= 0) & (col < NCOL)


def barrier(row, col, others):
    sem = pltpu.get_barrier_semaphore()
    for dr, dc in DIRS:

        @pl.when(inside(row + dr, col + dc))
        def _(dr=dr, dc=dc):
            pl.semaphore_signal(
                sem, inc=1, device_id=device_at(row + dr, col + dc), device_id_type=MESH_ID
            )

    for other in others:
        pl.semaphore_signal(sem, inc=1, device_id=other, device_id_type=MESH_ID)
    near = sum(inside(row + dr, col + dc).astype(jnp.int32) for dr, dc in DIRS)
    pl.semaphore_wait(sem, near + len(others))


def send_slices(dr, dc, first=1, count=TC):
    if dc == 0:
        src, dst = pl.ds(first, count), pl.ds(first, count)
    elif dc < 0:
        src, dst = pl.ds(1, 1), pl.ds(TC + 1, 1)
    else:
        src, dst = pl.ds(TC, 1), pl.ds(0, 1)
    return src, dst


def halo_copy(own, halo, dr, dc, send, recv, device, first=1, count=TC):
    src, dst = send_slices(dr, dc, first, count)
    if dr == 0:
        a, b = own.at[src], own.at[dst]
    elif dr < 0:
        a, b = own.at[src, 0:PATCH], halo.at[dst, PATCH : 2 * PATCH]
    else:
        a, b = own.at[src, PATCH : 2 * PATCH], halo.at[dst, 0:PATCH]
    return pltpu.make_async_remote_copy(
        src_ref=a, dst_ref=b, send_sem=send, recv_sem=recv, device_id=device, device_id_type=MESH_ID
    )


def mask_copy(mask, dr, dc, send, recv, device):
    src, dst = send_slices(dr, dc)
    if dr == 0:
        a, b = mask.at[0:2, src], mask.at[0:2, dst]
    elif dr < 0:
        a, b = mask.at[0:1, src], mask.at[3:4, dst]
    else:
        a, b = mask.at[1:2, src], mask.at[2:3, dst]
    return pltpu.make_async_remote_copy(
        src_ref=a, dst_ref=b, send_sem=send, recv_sem=recv, device_id=device, device_id_type=MESH_ID
    )


NT = (((1,), (1,)), ((), ()))
TN = (((0,), (0,)), ((), ()))


def eye(n):
    return lax.broadcasted_iota(jnp.int32, (n, n), 0) == lax.broadcasted_iota(jnp.int32, (n, n), 1)


def affinity(
    row, col, feat, tissue, e_ref, eh_ref, scale_ref, mine_ref, diag_ref, own, halo, mask, deg, served,
    fsend, frecv, csend, crecv, msend, mrecv, rsend, rrecv, ready, meanwhile,
):
    for k in (2, 3):
        mask[k] = jnp.zeros((TC + 2, 8, 128), jnp.float32)
    for k in (0, 1):
        mask[k, 0] = jnp.zeros((8, 128), jnp.float32)
        mask[k, TC + 1] = jnp.zeros((8, 128), jnp.float32)
        t = tissue[k].astype(jnp.float32)
        t = jnp.concatenate([t, t], axis=1)
        for c in range(TC):
            mask[k, c + 1] = jnp.broadcast_to(t[c : c + 1, :], (8, 128))

    def nothing(c, _):
        for side in (0, 1):
            eh_ref[side, c] = jnp.zeros((PATCH, 256), jnp.bfloat16)
        return 0

    lax.fori_loop(0, TC, nothing, 0, unroll=4)
    ready()

    there = [inside(row - 1, col), inside(row + 1, col)]
    device = [device_at(row - 1, col), device_at(row + 1, col)]

    def tile_copy(side, c):
        return pltpu.make_async_remote_copy(
            src_ref=own.at[c, side * PATCH : (side + 1) * PATCH],
            dst_ref=halo.at[c, (1 - side) * PATCH : (2 - side) * PATCH],
            send_sem=fsend.at[side, c],
            recv_sem=frecv.at[1 - side, c],
            device_id=device[side],
            device_id_type=MESH_ID,
        )

    def tile_arrival(side, c):
        return pltpu.make_async_remote_copy(
            src_ref=own.at[c, side * PATCH : (side + 1) * PATCH],
            dst_ref=halo.at[c, side * PATCH : (side + 1) * PATCH],
            send_sem=fsend.at[side, c],
            recv_sem=frecv.at[side, c],
            device_id=device[side],
            device_id_type=MESH_ID,
        )

    def weights_copy(side, c):
        return pltpu.make_async_remote_copy(
            src_ref=served.at[side, c - 1],
            dst_ref=eh_ref.at[1 - side, c - 1],
            send_sem=rsend.at[side, c],
            recv_sem=rrecv.at[1 - side, c],
            device_id=device[side],
            device_id_type=MESH_ID,
        )

    def weights_arrival(side, c):
        return pltpu.make_async_remote_copy(
            src_ref=served.at[side, c - 1],
            dst_ref=eh_ref.at[side, c - 1],
            send_sem=rsend.at[side, c],
            recv_sem=rrecv.at[side, c],
            device_id=device[side],
            device_id_type=MESH_ID,
        )

    crossing = (row == 3) | (row == 4)
    yields = [row == 4, row == 3]

    def on(side, fn):
        @pl.when(there[side])
        def _():
            fn()

    def early(side, fn):
        @pl.when(there[side] & jnp.logical_not(yields[side]))
        def _():
            fn()

    def normalise(c):
        for k in (0, 1):
            v = feat[k, c - 1].astype(jnp.float32)
            total = jnp.sum(v * v, axis=-1, keepdims=True)
            own[c, k * PATCH : (k + 1) * PATCH] = (v * lax.rsqrt(total + 1e-06)).astype(
                jnp.bfloat16
            )

    def side_copy(k):
        dr, dc = DIRS[k]
        return halo_copy(own, halo, dr, dc, csend.at[k], crecv.at[k], device_at(row, col + dc))

    def side_mask(k):
        dr, dc = DIRS[k]
        return mask_copy(mask, dr, dc, msend.at[k], mrecv.at[k], device_at(row + dr, col + dc))

    for k in range(4):
        dr, dc = DIRS[k]

        @pl.when(inside(row + dr, col + dc))
        def _(k=k):
            side_mask(k).start()

    half = TC // 2
    normalise(1)
    normalise(TC)
    normalise(2)
    for k in (2, 3):

        @pl.when(inside(row, col + DIRS[k][1]))
        def _(k=k):
            side_copy(k).start()

    normalise(TC - 1)
    for side in (0, 1):
        early(side, lambda side=side: (tile_copy(side, 1).start(), tile_copy(side, TC).start()))

    def group(g, _):
        normalise(g + 1)
        normalise(TC - g)
        early(0, lambda: tile_copy(0, TC + 1 - g).start())
        early(1, lambda: tile_copy(1, g).start())
        return 0

    lax.fori_loop(2, half, group, 0)
    early(0, lambda: tile_copy(0, half + 1).start())
    early(1, lambda: (tile_copy(1, half).start(), tile_copy(1, half + 1).start()))

    def arrived(k, fn):
        dr, dc = DIRS[k]

        @pl.when(inside(row - dr, col - dc))
        def _():
            fn()

    def sides():
        for k in (2, 3):
            arrived(k, lambda k=k: (side_mask(k).wait_recv(), side_copy(k).wait_recv()))

    up = [1] + list(range(TC, half, -1))
    down = [TC] + list(range(1, half + 2))

    lane = lax.broadcasted_iota(jnp.int32, (128, 128), 1)
    sub = lax.broadcasted_iota(jnp.int32, (128, 128), 0)
    diagonal = lane == sub
    first = lane[0:1] < PATCH

    def block(c, cc):
        s = lax.dot_general(own[c], own[cc], NT, preferred_element_type=jnp.float32)
        w = jnp.exp(AFFINITY_TEMP * (s - 1.0))
        m = jnp.where(first, mask[0, cc, 0:1], mask[1, cc, 0:1])
        return jnp.where(jnp.broadcast_to(m, (128, 128)) > 0.5, w, 0.0)

    def own_blocks(c):
        total = jnp.zeros((128, 1), jnp.float32)
        for d in range(3):
            w = block(c, c + d - 1)
            total = total + jnp.sum(w, axis=1, keepdims=True)
            if d == 1:
                self_w = jnp.sum(jnp.where(diagonal, w, 0.0), axis=1, keepdims=True)
                diag_ref[c - 1] = jnp.broadcast_to(self_w, (128, 128))
                w = jnp.where(diagonal, 0.0, w)
            e_ref[c - 1, :, d * 128 : (d + 1) * 128] = w.astype(jnp.bfloat16)
        deg[c] = jnp.broadcast_to(total, (128, 128))

    meanwhile()

    def rows_of(left, right, right_mask, c):
        s = lax.dot_general(left, right, NT, preferred_element_type=jnp.float32)
        w = jnp.exp(AFFINITY_TEMP * (s - 1.0))
        m0 = jnp.where(first, mask[right_mask, c - 1, 0:1], mask[right_mask, c, 0:1])
        m1 = mask[right_mask, c + 1, 0:1]
        w0 = jnp.where(jnp.broadcast_to(m0, (PATCH, 128)) > 0.5, w[:, :128], 0.0)
        w1 = jnp.where(jnp.broadcast_to(m1[:, :PATCH], (PATCH, PATCH)) > 0.5, w[:, 128:], 0.0)
        w1 = jnp.concatenate([w1, jnp.zeros((PATCH, PATCH), jnp.float32)], axis=1)
        return jnp.concatenate([w0, w1], axis=1).astype(jnp.bfloat16)

    def near(ref, side, c):
        return ref[pl.ds(c - 1, 3), side * PATCH : (side + 1) * PATCH].reshape(3 * PATCH, -1)

    def serve(side, c, wait=True):
        if wait:
            tile_arrival(side, c).wait_recv()
        left = halo[c, side * PATCH : (side + 1) * PATCH]
        served[side, c - 1] = rows_of(left, near(own, side, c), side, c)
        weights_copy(side, c).start()

    def at_home(side, c):
        left = own[c, side * PATCH : (side + 1) * PATCH]
        eh_ref[side, c - 1] = rows_of(left, near(halo, side, c), 2 + side, c)

    def inner(c, _):
        own_blocks(c)
        return 0

    lax.fori_loop(2, 6, inner, 0)
    @pl.when(crossing)
    def _():
        sides()

    for side, columns in ((0, up), (1, down)):

        @pl.when(yields[side])
        def _(side=side, columns=columns):
            for c in columns:
                tile_copy(side, c).start()

    for k in (0, 1):
        arrived(k, lambda k=k: side_mask(k).wait_recv())
    on(0, lambda: serve(0, 2))
    on(1, lambda: serve(1, TC - 1))

    def arrive(g, _):
        on(0, lambda: serve(0, g + 1))
        on(1, lambda: serve(1, TC - g))

        @pl.when(g == LATE)
        def _():
            @pl.when(jnp.logical_not(crossing))
            def _():
                sides()

            for c in (1, TC):
                for side in (0, 1):
                    on(side, lambda side=side, c=c: serve(side, c, c != (1, TC)[side]))

        @pl.when(g == 2)
        def _():
            for side in (0, 1):
                on(side, lambda side=side: (tile_arrival(side, (1, TC)[side]).wait_recv()))

        on(0, lambda: at_home(0, g))
        on(1, lambda: at_home(1, TC + 1 - g))

        @pl.when(g < 7)
        def _():
            own_blocks(2 * g + 2)
            own_blocks(2 * g + 3)

        @pl.when(g == 7)
        def _():
            own_blocks(1)
            own_blocks(TC)

        return 0

    lax.fori_loop(2, half, arrive, 0)
    on(0, lambda: (serve(0, half + 1), at_home(0, half)))

    def finish(c):
        eh = jnp.concatenate([eh_ref[0, c - 1], eh_ref[1, c - 1]], axis=0).astype(jnp.float32)
        total = deg[c][:, 0:1] + jnp.sum(eh, axis=1, keepdims=True)
        m = jnp.where(first, mask[0, c, 0:1], mask[1, c, 0:1])
        mine = jnp.sum(jnp.where(diagonal, jnp.broadcast_to(m, (128, 128)), 0.0), axis=1, keepdims=True)
        scale = lax.rsqrt(1.0 + mine * total)
        self_w = diag_ref[c - 1]
        scale_ref[c - 1] = jnp.broadcast_to(scale, (128, 128))
        mine_ref[c - 1] = jnp.broadcast_to(scale * mine, (128, 128))
        diag_ref[c - 1] = 1.0 + (mine * scale * scale) * self_w

    def back(side, columns):
        for c in columns:
            weights_arrival(side, c).wait_recv()

    on(0, lambda: back(0, up))
    on(1, lambda: back(1, down))

    def finish_one(c, _):
        finish(c)
        return 0

    lax.fori_loop(1, TC + 1, finish_one, 0, unroll=4)

    def sent():
        for side, mine, theirs in ((0, up, down), (1, down, up)):

            def go(side=side, mine=mine, theirs=theirs):
                for c in mine:
                    tile_copy(side, c).wait_send()
                for c in theirs:
                    weights_copy(side, c).wait_send()

            on(side, go)
        for k in range(4):
            dr, dc = DIRS[k]

            @pl.when(inside(row + dr, col + dc))
            def _(k=k):
                side_mask(k).wait_send()
                if k >= 2:
                    side_copy(k).wait_send()

    return sent


def stage_peers(pos):
    z = pos[3] * 2 + pos[0]
    core = (pos[4], [(pos[0], pos[1], pos[2], pos[3], 1 - pos[4])])
    x = (pos[1], [(pos[0], (pos[1] + d) % 4, pos[2], pos[3], pos[4]) for d in (1, 2, 3)])
    y = (pos[2], [(pos[0], pos[1], (pos[2] + d) % 4, pos[3], pos[4]) for d in (1, 2, 3)])
    along = [(z + d) % 4 for d in (1, 2, 3)]
    zz = (z, [(q % 2, pos[1], pos[2], q // 2, pos[4]) for q in along])
    return [core, y, zz, x]


def inverse_factor(gram):
    n = RANK
    m = jnp.concatenate([gram, jnp.where(eye(n), 1.0, 0.0)], axis=1)
    sub = lax.broadcasted_iota(jnp.int32, (n, 2 * n), 0)
    lane = lax.broadcasted_iota(jnp.int32, (n, 2 * n), 1)
    for k in range(n - 1):
        column = jnp.broadcast_to(m[:, k : k + 1], (n, 2 * n))
        pivot = column[k : k + 1, :]
        line = m[k : k + 1, :] / pivot
        m = m - jnp.where(sub > k, column, 0.0) * line
    d = jnp.sum(jnp.where(lane == sub, m, 0.0), axis=1, keepdims=True)
    return m[:, n:] * lax.rsqrt(d)


def pair_of(v, low):
    hi = v.astype(jnp.bfloat16)
    lo = (v - hi.astype(jnp.float32)).astype(jnp.bfloat16)
    return jnp.where(low, hi, lo)


def kernel(
    feat, tissue, probe, out_ref,
    ufeat, hfeat, mask, deg, served, e_ref, eh_ref, scale_ref, mine_ref, diag_ref,
    own, halo, acc, y, pair, total, gsum,
    fsend, frecv, csend, crecv, msend, mrecv, rsend, rrecv, psend, precv, gsend, grecv,
):
    pos = position()
    row, col = row_col(pos)
    stages = stage_peers(pos)
    low = lax.broadcasted_iota(jnp.int32, (128, 128), 1) < RANK
    zero = jnp.zeros((128, 128), jnp.bfloat16)

    def clear(i, _):
        own[i, 0] = zero
        own[i, TC + 1] = zero

        def one(c, _):
            for side in (0, 1):
                halo[i, side, c] = zero[:PATCH]
            return 0

        lax.fori_loop(0, TC + 3, one, 0)
        return 0

    lax.fori_loop(0, ITERS, clear, 0)

    def ready():
        barrier(row, col, [p for _, peers in stages for p in peers])

    def meanwhile():
        def load(c, _):
            for k in (0, 1):
                v = probe[k, c]
                y[c, k * PATCH : (k + 1) * PATCH] = jnp.concatenate([v, v], axis=1)
            return 0

        lax.fori_loop(0, TC, load, 0, unroll=4)

    sent = affinity(
        row, col, feat, tissue, e_ref, eh_ref, scale_ref, mine_ref, diag_ref, ufeat, hfeat, mask,
        deg, served, fsend, frecv, csend, crecv, msend, mrecv, rsend, rrecv, ready, meanwhile,
    )

    def panel(t, k):
        dr, dc = DIRS[k]
        src, dst = send_slices(dr, dc)
        if dr == 0:
            a, b = own.at[t, src], own.at[t, dst]
        elif dr < 0:
            a, b = own.at[t, src, 0:PATCH], halo.at[t, 1, dst]
        else:
            a, b = own.at[t, src, PATCH : 2 * PATCH], halo.at[t, 0, dst]
        return pltpu.make_async_remote_copy(
            src_ref=a, dst_ref=b, send_sem=psend.at[t, k], recv_sem=precv.at[t, k],
            device_id=device_at(row + dr, col + dc), device_id_type=MESH_ID,
        )

    def each_target(fn):
        for k, (dr, dc) in enumerate(DIRS):

            @pl.when(inside(row + dr, col + dc))
            def _(k=k):
                fn(k)

    def each_source(fn):
        for k, (dr, dc) in enumerate(DIRS):

            @pl.when(inside(row - dr, col - dc))
            def _(k=k):
                fn(k)

    def own_part(t, first, stop):
        def go(c, _):
            b = own[t, pl.ds(c, 3)].reshape(384, 128)
            acc[c] = jnp.dot(e_ref[c], b, preferred_element_type=jnp.float32)
            return 0

        lax.fori_loop(first, stop, go, 0, unroll=stop - first)

    def product(t, c):
        v = [
            jnp.dot(
                eh_ref[side, c],
                halo[t, side, pl.ds(c, 4)].reshape(256, 128),
                preferred_element_type=jnp.float32,
            )
            for side in (0, 1)
        ]
        v = acc[c] + jnp.concatenate(v, axis=0)
        v = v + pltpu.roll(v, RANK, 1)
        return y[c] * diag_ref[c] + mine_ref[c] * v

    def start_stage(t, s, packed):
        place, peers = stages[s]
        gsum[t, s, place] = packed
        for d, there in enumerate(peers):
            pltpu.make_async_remote_copy(
                src_ref=gsum.at[t, s, place],
                dst_ref=gsum.at[t, s, place],
                send_sem=gsend.at[t, s, d],
                recv_sem=grecv.at[t, s, d],
                device_id=there,
                device_id_type=MESH_ID,
            ).start()

    def end_stage(t, s):
        place, peers = stages[s]
        n = len(peers) + 1
        for d, there in enumerate(peers):
            pltpu.make_async_remote_copy(
                src_ref=gsum.at[t, s, place],
                dst_ref=gsum.at[t, s, (place + n - 1 - d) % n],
                send_sem=gsend.at[t, s, d],
                recv_sem=grecv.at[t, s, d],
                device_id=there,
                device_id_type=MESH_ID,
            ).wait_recv()
        packed = gsum[t, s, 0]
        for i in range(1, n):
            packed = packed + gsum[t, s, i]
        return packed

    def new_rows(t, c, v):
        p = pair_of(v, low)
        total[...] += lax.dot_general(p, p, TN, preferred_element_type=jnp.float32)
        if t < ITERS - 1:
            y[c] = v
            own[t + 1, c + 1] = pair_of(v * scale_ref[c], low)
        else:
            pair[c] = p

    def solver(packed):
        gram = jnp.concatenate([packed[:, :64], packed[:, 64:]], axis=0)
        inv = inverse_factor(gram)
        hi = inv.astype(jnp.bfloat16)
        lo = (inv - hi.astype(jnp.float32)).astype(jnp.bfloat16)
        both = jnp.concatenate([hi, hi, lo, lo], axis=1)
        both = jnp.concatenate([both, both], axis=0)

        def solve(p):
            p = jnp.concatenate([p, p], axis=1)
            return lax.dot_general(p, both, NT, preferred_element_type=jnp.float32)

        return solve

    def first(c, _):
        own[0, c + 1] = pair_of(y[c] * scale_ref[c], low)
        return 0

    lax.fori_loop(0, TC, first, 0, unroll=4)
    each_target(lambda k: panel(0, k).start())
    own_part(0, 1, TC - 1)
    each_source(lambda k: panel(0, k).wait_recv())
    own_part(0, 0, 1)
    own_part(0, TC - 1, TC)
    total[...] = jnp.zeros((128, 128), jnp.float32)

    def rows0(c, _):
        new_rows(0, c, product(0, c))
        return 0

    lax.fori_loop(0, TC, rows0, 0, unroll=8)

    solve = None
    for t in range(ITERS):
        g = total[...]
        g = g[:, :64] + g[:, 64:]
        g = g[:64] + g[64:]
        packed = jnp.concatenate([g[:32], g[32:]], axis=1)
        more = t < ITERS - 1
        start_stage(t, 0, packed)
        if more:
            each_target(lambda k: panel(t + 1, k).start())
            own_part(t + 1, 1, 5)
        start_stage(t, 1, end_stage(t, 0))
        if more:
            own_part(t + 1, 5, 10)
        start_stage(t, 2, end_stage(t, 1))
        if more:
            own_part(t + 1, 10, TC - 1)
        start_stage(t, 3, end_stage(t, 2))
        if more:
            each_source(lambda k: panel(t + 1, k).wait_recv())
            own_part(t + 1, 0, 1)
            own_part(t + 1, TC - 1, TC)

            def apply(c, _):
                pair[c] = pair_of(product(t + 1, c), low)
                return 0

            lax.fori_loop(0, TC, apply, 0, unroll=8)
        solve = solver(end_stage(t, 3))
        if more:
            total[...] = jnp.zeros((128, 128), jnp.float32)

            def rows(c, _):
                new_rows(t + 1, c, solve(pair[c]))
                return 0

            lax.fori_loop(0, TC, rows, 0, unroll=8)

    factor = math.sqrt(float(NROW * 2 * NCOL * TC * PATCH))

    def last(c, _):
        v = factor * solve(pair[c])
        for k in (0, 1):
            out_ref[k, c] = v[k * PATCH : (k + 1) * PATCH, :RANK]
        return 0

    lax.fori_loop(0, TC, last, 0, unroll=4)

    sent()
    for t in range(ITERS):
        each_target(lambda k: panel(t, k).wait_send())
        for s, (place, peers) in enumerate(stages):
            for d, there in enumerate(peers):
                pltpu.make_async_remote_copy(
                    src_ref=gsum.at[t, s, place],
                    dst_ref=gsum.at[t, s, place],
                    send_sem=gsend.at[t, s, d],
                    recv_sem=grecv.at[t, s, d],
                    device_id=there,
                    device_id_type=MESH_ID,
                ).wait_send()


VM = pl.BlockSpec(memory_space=pltpu.VMEM)
DMA = pltpu.SemaphoreType.DMA
LIMIT = 60 * 2**20


def local(features, tissue, probe):
    width = features.shape[-1]
    full = (TC, 128, 128)
    wide = (TC + 2, 128, width)
    out = pl.pallas_call(
        kernel,
        out_shape=jax.ShapeDtypeStruct((2, TC, PATCH, RANK), jnp.float32),
        in_specs=[VM] * 3,
        out_specs=VM,
        scratch_shapes=[
            pltpu.VMEM(wide, jnp.bfloat16),
            pltpu.VMEM(wide, jnp.bfloat16),
            pltpu.VMEM((4, TC + 2, 8, 128), jnp.float32),
            pltpu.VMEM((TC + 1, 128, 128), jnp.float32),
            pltpu.VMEM((2, TC, PATCH, 256), jnp.bfloat16),
            pltpu.VMEM((TC, 128, 384), jnp.bfloat16),
            pltpu.VMEM((2, TC, PATCH, 256), jnp.bfloat16),
            pltpu.VMEM(full, jnp.float32),
            pltpu.VMEM(full, jnp.float32),
            pltpu.VMEM(full, jnp.float32),
            pltpu.VMEM((ITERS, TC + 2, 128, 128), jnp.bfloat16),
            pltpu.VMEM((ITERS, 2, TC + 3, PATCH, 128), jnp.bfloat16),
            pltpu.VMEM(full, jnp.float32),
            pltpu.VMEM(full, jnp.float32),
            pltpu.VMEM(full, jnp.bfloat16),
            pltpu.VMEM((128, 128), jnp.float32),
            pltpu.VMEM((ITERS, 4, 4, 32, 128), jnp.float32),
            DMA((2, TC + 1)), DMA((2, TC + 1)), DMA((4,)), DMA((4,)), DMA((4,)), DMA((4,)),
            DMA((2, TC + 1)), DMA((2, TC + 1)),
            DMA((ITERS, 8)), DMA((ITERS, 8)), DMA((ITERS, 4, 3)), DMA((ITERS, 4, 3)),
        ],
        compiler_params=pltpu.CompilerParams(
            collective_id=0, has_side_effects=True, vmem_limit_bytes=LIMIT
        ),
        name="range_finder",
    )(features, tissue, probe.reshape(2, TC, PATCH, RANK))
    return out.reshape(2, TC, PATCH * RANK)


def solution(mesh):
    torus = Mesh(mesh.devices.reshape(2, 4, 4, 2, 2), AXES)
    return jax.shard_map(
        local,
        mesh=torus,
        in_specs=(P(ROW, COL, None, None), P(ROW, COL, None), P(ROW, COL, None)),
        out_specs=P(ROW, COL, None),
        check_vma=False,
    )
```

```python
import functools
import math

import jax
import jax.numpy as jnp
from jax import lax
from jax.experimental import pallas as pl
from jax.experimental.pallas import tpu as pltpu
from jax.sharding import Mesh
from jax.sharding import PartitionSpec as P

RANK = 64
ITERS = 3
PATCH = 64
AXES = ("row_0", "row_1", "col_0", "col_1", "col_2")
ROW = ("row_0", "row_1")
COL = ("col_0", "col_1", "col_2")
NROW, NCOL = 8, 16
TC = 16
MESH_ID = pl.DeviceIdType.MESH
AFFINITY_TEMP = 4.0

DIRS = ((-1, 0), (1, 0), (0, -1), (0, 1), (-1, -1), (-1, 1), (1, -1), (1, 1))


def position():
    return tuple(lax.axis_index(a) for a in AXES)


def row_col(pos):
    return pos[0] * 4 + pos[1], pos[2] * 4 + pos[3] * 2 + pos[4]


def device_at(row, col):
    row = jnp.clip(row, 0, NROW - 1)
    col = jnp.clip(col, 0, NCOL - 1)
    return (row // 4, row % 4, col // 4, (col // 2) % 2, col % 2)


def inside(row, col):
    return (row >= 0) & (row < NROW) & (col >= 0) & (col < NCOL)


def barrier(row, col, others):
    sem = pltpu.get_barrier_semaphore()
    for dr, dc in DIRS:

        @pl.when(inside(row + dr, col + dc))
        def _(dr=dr, dc=dc):
            pl.semaphore_signal(
                sem, inc=1, device_id=device_at(row + dr, col + dc), device_id_type=MESH_ID
            )

    for other in others:
        pl.semaphore_signal(sem, inc=1, device_id=other, device_id_type=MESH_ID)
    near = sum(inside(row + dr, col + dc).astype(jnp.int32) for dr, dc in DIRS)
    pl.semaphore_wait(sem, near + len(others))


def send_slices(dr, dc, first=1, count=TC):
    if dc == 0:
        src, dst = pl.ds(first, count), pl.ds(first, count)
    elif dc < 0:
        src, dst = pl.ds(1, 1), pl.ds(TC + 1, 1)
    else:
        src, dst = pl.ds(TC, 1), pl.ds(0, 1)
    return src, dst


def halo_copy(own, halo, dr, dc, send, recv, device, first=1, count=TC):
    src, dst = send_slices(dr, dc, first, count)
    if dr == 0:
        a, b = own.at[src], own.at[dst]
    elif dr < 0:
        a, b = own.at[src, 0:PATCH], halo.at[dst, PATCH : 2 * PATCH]
    else:
        a, b = own.at[src, PATCH : 2 * PATCH], halo.at[dst, 0:PATCH]
    return pltpu.make_async_remote_copy(
        src_ref=a, dst_ref=b, send_sem=send, recv_sem=recv, device_id=device, device_id_type=MESH_ID
    )


def mask_copy(mask, dr, dc, send, recv, device):
    src, dst = send_slices(dr, dc)
    if dr == 0:
        a, b = mask.at[0:2, src], mask.at[0:2, dst]
    elif dr < 0:
        a, b = mask.at[0:1, src], mask.at[3:4, dst]
    else:
        a, b = mask.at[1:2, src], mask.at[2:3, dst]
    return pltpu.make_async_remote_copy(
        src_ref=a, dst_ref=b, send_sem=send, recv_sem=recv, device_id=device, device_id_type=MESH_ID
    )


NT = (((1,), (1,)), ((), ()))
TN = (((0,), (0,)), ((), ()))


def eye(n):
    return lax.broadcasted_iota(jnp.int32, (n, n), 0) == lax.broadcasted_iota(jnp.int32, (n, n), 1)


def affinity(
    row, col, feat, tissue, e_ref, eh_ref, scale_ref, mine_ref, diag_ref, own, halo, mask, deg, served,
    fsend, frecv, csend, crecv, msend, mrecv, rsend, rrecv, ready, meanwhile, load_feat,
):
    for k in (2, 3):
        mask[k] = jnp.zeros((TC + 2, 8, 128), jnp.float32)
    for k in (0, 1):
        mask[k, 0] = jnp.zeros((8, 128), jnp.float32)
        mask[k, TC + 1] = jnp.zeros((8, 128), jnp.float32)
        t = tissue[k].astype(jnp.float32)
        t = jnp.concatenate([t, t], axis=1)
        for c in range(TC):
            mask[k, c + 1] = jnp.broadcast_to(t[c : c + 1, :], (8, 128))

    def nothing(c, _):
        for side in (0, 1):
            eh_ref[side, c] = jnp.zeros((PATCH, 256), jnp.bfloat16)
        return 0

    lax.fori_loop(0, TC, nothing, 0, unroll=4)
    ready()

    there = [inside(row - 1, col), inside(row + 1, col)]
    device = [device_at(row - 1, col), device_at(row + 1, col)]

    def tile_copy(side, c):
        return pltpu.make_async_remote_copy(
            src_ref=own.at[c, side * PATCH : (side + 1) * PATCH],
            dst_ref=halo.at[c, (1 - side) * PATCH : (2 - side) * PATCH],
            send_sem=fsend.at[side, c],
            recv_sem=frecv.at[1 - side, c],
            device_id=device[side],
            device_id_type=MESH_ID,
        )

    def tile_arrival(side, c):
        return pltpu.make_async_remote_copy(
            src_ref=own.at[c, side * PATCH : (side + 1) * PATCH],
            dst_ref=halo.at[c, side * PATCH : (side + 1) * PATCH],
            send_sem=fsend.at[side, c],
            recv_sem=frecv.at[side, c],
            device_id=device[side],
            device_id_type=MESH_ID,
        )

    def weights_copy(side, c):
        return pltpu.make_async_remote_copy(
            src_ref=served.at[side, c - 1],
            dst_ref=eh_ref.at[1 - side, c - 1],
            send_sem=rsend.at[side, c],
            recv_sem=rrecv.at[1 - side, c],
            device_id=device[side],
            device_id_type=MESH_ID,
        )

    def weights_arrival(side, c):
        return pltpu.make_async_remote_copy(
            src_ref=served.at[side, c - 1],
            dst_ref=eh_ref.at[side, c - 1],
            send_sem=rsend.at[side, c],
            recv_sem=rrecv.at[side, c],
            device_id=device[side],
            device_id_type=MESH_ID,
        )

    crossing = (row == 3) | (row == 4)
    yields = [row == 4, row == 3]

    def on(side, fn):
        @pl.when(there[side])
        def _():
            fn()

    def early(side, fn):
        @pl.when(there[side] & jnp.logical_not(yields[side]))
        def _():
            fn()

    def normalise(c):
        load_feat(c).wait()
        for k in (0, 1):
            v = feat[k, c - 1].astype(jnp.float32)
            total = jnp.sum(v * v, axis=-1, keepdims=True)
            own[c, k * PATCH : (k + 1) * PATCH] = (v * lax.rsqrt(total + 1e-06)).astype(
                jnp.bfloat16
            )

    def side_copy(k):
        dr, dc = DIRS[k]
        return halo_copy(own, halo, dr, dc, csend.at[k], crecv.at[k], device_at(row, col + dc))

    def side_mask(k):
        dr, dc = DIRS[k]
        return mask_copy(mask, dr, dc, msend.at[k], mrecv.at[k], device_at(row + dr, col + dc))

    for k in range(4):
        dr, dc = DIRS[k]

        @pl.when(inside(row + dr, col + dc))
        def _(k=k):
            side_mask(k).start()

    half = TC // 2
    normalise(1)
    normalise(TC)
    normalise(2)
    for k in (2, 3):

        @pl.when(inside(row, col + DIRS[k][1]))
        def _(k=k):
            side_copy(k).start()

    normalise(TC - 1)
    for side in (0, 1):
        early(side, lambda side=side: (tile_copy(side, 1).start(), tile_copy(side, TC).start()))

    def group(g, _):
        normalise(g + 1)
        normalise(TC - g)
        early(0, lambda: tile_copy(0, TC + 1 - g).start())
        early(1, lambda: tile_copy(1, g).start())
        return 0

    lax.fori_loop(2, half, group, 0)
    early(0, lambda: tile_copy(0, half + 1).start())
    early(1, lambda: (tile_copy(1, half).start(), tile_copy(1, half + 1).start()))

    def arrived(k, fn):
        dr, dc = DIRS[k]

        @pl.when(inside(row - dr, col - dc))
        def _():
            fn()

    def sides():
        for k in (2, 3):
            arrived(k, lambda k=k: (side_mask(k).wait_recv(), side_copy(k).wait_recv()))

    up = [1] + list(range(TC, half, -1))
    down = [TC] + list(range(1, half + 2))

    lane = lax.broadcasted_iota(jnp.int32, (128, 128), 1)
    sub = lax.broadcasted_iota(jnp.int32, (128, 128), 0)
    diagonal = lane == sub
    first = lane[0:1] < PATCH

    def block(c, cc):
        s = lax.dot_general(own[c], own[cc], NT, preferred_element_type=jnp.float32)
        w = jnp.exp(AFFINITY_TEMP * (s - 1.0))
        m = jnp.where(first, mask[0, cc, 0:1], mask[1, cc, 0:1])
        return jnp.where(jnp.broadcast_to(m, (128, 128)) > 0.5, w, 0.0)

    def own_blocks(c):
        total = jnp.zeros((128, 1), jnp.float32)
        for d in range(3):
            w = block(c, c + d - 1)
            total = total + jnp.sum(w, axis=1, keepdims=True)
            if d == 1:
                self_w = jnp.sum(jnp.where(diagonal, w, 0.0), axis=1, keepdims=True)
                diag_ref[c - 1] = jnp.broadcast_to(self_w, (128, 128))
                w = jnp.where(diagonal, 0.0, w)
            e_ref[c - 1, :, d * 128 : (d + 1) * 128] = w.astype(jnp.bfloat16)
        deg[c] = jnp.broadcast_to(total, (128, 128))

    meanwhile()

    def rows_of(left, right, right_mask, c):
        s = lax.dot_general(left, right, NT, preferred_element_type=jnp.float32)
        w = jnp.exp(AFFINITY_TEMP * (s - 1.0))
        m0 = jnp.where(first, mask[right_mask, c - 1, 0:1], mask[right_mask, c, 0:1])
        m1 = mask[right_mask, c + 1, 0:1]
        w0 = jnp.where(jnp.broadcast_to(m0, (PATCH, 128)) > 0.5, w[:, :128], 0.0)
        w1 = jnp.where(jnp.broadcast_to(m1[:, :PATCH], (PATCH, PATCH)) > 0.5, w[:, 128:], 0.0)
        w1 = jnp.concatenate([w1, jnp.zeros((PATCH, PATCH), jnp.float32)], axis=1)
        return jnp.concatenate([w0, w1], axis=1).astype(jnp.bfloat16)

    def near(ref, side, c):
        return ref[pl.ds(c - 1, 3), side * PATCH : (side + 1) * PATCH].reshape(3 * PATCH, -1)

    def serve(side, c, wait=True):
        if wait:
            tile_arrival(side, c).wait_recv()
        left = halo[c, side * PATCH : (side + 1) * PATCH]
        served[side, c - 1] = rows_of(left, near(own, side, c), side, c)
        weights_copy(side, c).start()

    def at_home(side, c):
        left = own[c, side * PATCH : (side + 1) * PATCH]
        eh_ref[side, c - 1] = rows_of(left, near(halo, side, c), 2 + side, c)

    def inner(c, _):
        own_blocks(c)
        return 0

    lax.fori_loop(2, 6, inner, 0)
    @pl.when(crossing)
    def _():
        sides()

    for side, columns in ((0, up), (1, down)):

        @pl.when(yields[side])
        def _(side=side, columns=columns):
            for c in columns:
                tile_copy(side, c).start()

    for k in (0, 1):
        arrived(k, lambda k=k: side_mask(k).wait_recv())
    on(0, lambda: serve(0, 2))
    on(1, lambda: serve(1, TC - 1))

    def arrive(g, _):
        on(0, lambda: serve(0, g + 1))
        on(1, lambda: serve(1, TC - g))

        @pl.when(g == 2)
        def _():
            for side in (0, 1):
                on(side, lambda side=side: (tile_arrival(side, (1, TC)[side]).wait_recv()))

        on(0, lambda: at_home(0, g))
        on(1, lambda: at_home(1, TC + 1 - g))

        @pl.when(g < 7)
        def _():
            own_blocks(2 * g + 2)
            own_blocks(2 * g + 3)

        return 0

    lax.fori_loop(2, half, arrive, 0)
    on(0, lambda: (serve(0, half + 1), at_home(0, half)))

    @pl.when(jnp.logical_not(crossing))
    def _():
        sides()

    for c in (1, TC):
        for side in (0, 1):
            on(side, lambda side=side, c=c: serve(side, c, c != (1, TC)[side]))
    for c in (1, TC):
        own_blocks(c)

    def finish(c):
        eh = jnp.concatenate([eh_ref[0, c - 1], eh_ref[1, c - 1]], axis=0).astype(jnp.float32)
        total = deg[c][:, 0:1] + jnp.sum(eh, axis=1, keepdims=True)
        m = jnp.where(first, mask[0, c, 0:1], mask[1, c, 0:1])
        mine = jnp.sum(jnp.where(diagonal, jnp.broadcast_to(m, (128, 128)), 0.0), axis=1, keepdims=True)
        scale = lax.rsqrt(1.0 + mine * total)
        self_w = diag_ref[c - 1]
        scale_ref[c - 1] = jnp.broadcast_to(scale, (128, 128))
        mine_ref[c - 1] = jnp.broadcast_to(scale * mine, (128, 128))
        diag_ref[c - 1] = 1.0 + (mine * scale * scale) * self_w

    def back(side, columns):
        for c in columns:
            weights_arrival(side, c).wait_recv()

    on(0, lambda: back(0, up))
    on(1, lambda: back(1, down))

    def finish_one(c, _):
        finish(c)
        return 0

    lax.fori_loop(1, TC + 1, finish_one, 0, unroll=4)

    def sent():
        for side, mine, theirs in ((0, up, down), (1, down, up)):

            def go(side=side, mine=mine, theirs=theirs):
                for c in mine:
                    tile_copy(side, c).wait_send()
                for c in theirs:
                    weights_copy(side, c).wait_send()

            on(side, go)
        for k in range(4):
            dr, dc = DIRS[k]

            @pl.when(inside(row + dr, col + dc))
            def _(k=k):
                side_mask(k).wait_send()
                if k >= 2:
                    side_copy(k).wait_send()

    return sent


def stage_peers(pos):
    z = pos[3] * 2 + pos[0]
    core = (pos[4], [(pos[0], pos[1], pos[2], pos[3], 1 - pos[4])])
    x = (pos[1], [(pos[0], (pos[1] + d) % 4, pos[2], pos[3], pos[4]) for d in (1, 2, 3)])
    y = (pos[2], [(pos[0], pos[1], (pos[2] + d) % 4, pos[3], pos[4]) for d in (1, 2, 3)])
    along = [(z + d) % 4 for d in (1, 2, 3)]
    zz = (z, [(q % 2, pos[1], pos[2], q // 2, pos[4]) for q in along])
    return [core, y, zz, x]


def inverse_factor(gram):
    n = RANK
    row_block = 8
    on_diagonal = jnp.where(eye(n), gram, 0.0)
    by_row = lax.rsqrt(jnp.sum(on_diagonal, axis=1, keepdims=True))
    by_lane = lax.rsqrt(jnp.sum(on_diagonal, axis=0, keepdims=True))
    start = jnp.concatenate([gram * by_row * by_lane, jnp.where(eye(n), by_lane, 0.0)], axis=1)
    m = [start[q : q + row_block] for q in range(0, n, row_block)]
    sub = lax.broadcasted_iota(jnp.int32, (row_block, 2 * n), 0)
    for k in range(0, n, 2):
        j, i = divmod(k, row_block)
        left = [jnp.broadcast_to(m[q][:, k : k + 1], (row_block, 2 * n)) for q in range(j, len(m))]
        right = [
            jnp.broadcast_to(m[q][:, k + 1 : k + 2], (row_block, 2 * n)) for q in range(j, len(m))
        ]
        r0, r1 = m[j][i : i + 1], m[j][i + 1 : i + 2]
        a, b, d = left[0][i : i + 1], left[0][i + 1 : i + 2], right[0][i + 1 : i + 2]
        inv = 1.0 / (a * d - b * b)
        u0 = (d * r0 - b * r1) * inv
        u1 = (a * r1 - b * r0) * inv
        second = r1 - (b / a) * r0
        for q in range(j, len(m)):
            new = m[q] - (left[q - j] * u0 + right[q - j] * u1)
            if q == j:
                new = jnp.where(sub > i + 1, new, m[q])
                new = jnp.where(sub == i + 1, second, new)
            m[q] = new
    m = jnp.concatenate(m, axis=0)
    d = jnp.sum(jnp.where(eye(n), m[:, :n], 0.0), axis=1, keepdims=True)
    return m[:, n:] * lax.rsqrt(d)


def pair_of(v, low):
    hi = v.astype(jnp.bfloat16)
    lo = (v - hi.astype(jnp.float32)).astype(jnp.bfloat16)
    return jnp.where(low, hi, lo)


def kernel(
    feat_hbm, tissue, probe, out_ref,
    feat, ufeat, hfeat, mask, deg, served, e_ref, eh_ref, scale_ref, mine_ref, diag_ref,
    own, halo, acc, y, pair, total, gsum,
    fsend, frecv, csend, crecv, msend, mrecv, rsend, rrecv, psend, precv, gsend, grecv, isem,
):
    def load_feat(c):
        return pltpu.make_async_copy(
            feat_hbm.at[:, pl.ds(c - 1, 1)], feat.at[:, pl.ds(c - 1, 1)], isem.at[c]
        )

    for c in range(1, TC // 2 + 1):
        load_feat(c).start()
        load_feat(TC + 1 - c).start()

    pos = position()
    row, col = row_col(pos)
    stages = stage_peers(pos)
    low = lax.broadcasted_iota(jnp.int32, (128, 128), 1) < RANK
    lane_low = lax.broadcasted_iota(jnp.int32, (PATCH, 128), 1) < RANK
    zero = jnp.zeros((128, 128), jnp.bfloat16)

    def clear(i, _):
        own[i, 0] = zero
        own[i, TC + 1] = zero

        def one(c, _):
            for side in (0, 1):
                halo[i, side, c] = zero[:PATCH]
            return 0

        lax.fori_loop(0, TC + 3, one, 0)
        return 0

    lax.fori_loop(0, ITERS, clear, 0)

    def ready():
        barrier(row, col, [p for _, peers in stages for p in peers])

    def meanwhile():
        def load(c, _):
            for k in (0, 1):
                v = probe[k, c]
                w = pltpu.roll(v, RANK, 1)
                even = lane_low[: PATCH // 2]
                y[c, pl.ds(k * PATCH, PATCH // 2, stride=2)] = jnp.where(even, v, w)
                y[c, pl.ds(k * PATCH + 1, PATCH // 2, stride=2)] = jnp.where(even, w, v)
            return 0

        lax.fori_loop(0, TC, load, 0, unroll=4)

    sent = affinity(
        row, col, feat, tissue, e_ref, eh_ref, scale_ref, mine_ref, diag_ref, ufeat, hfeat, mask,
        deg, served, fsend, frecv, csend, crecv, msend, mrecv, rsend, rrecv, ready, meanwhile, load_feat,
    )

    def panel(t, k):
        dr, dc = DIRS[k]
        src, dst = send_slices(dr, dc)
        if dr == 0:
            a, b = own.at[t, src], own.at[t, dst]
        elif dr < 0:
            a, b = own.at[t, src, 0:PATCH], halo.at[t, 1, dst]
        else:
            a, b = own.at[t, src, PATCH : 2 * PATCH], halo.at[t, 0, dst]
        return pltpu.make_async_remote_copy(
            src_ref=a, dst_ref=b, send_sem=psend.at[t, k], recv_sem=precv.at[t, k],
            device_id=device_at(row + dr, col + dc), device_id_type=MESH_ID,
        )

    def each_target(fn):
        for k, (dr, dc) in enumerate(DIRS):

            @pl.when(inside(row + dr, col + dc))
            def _(k=k):
                fn(k)

    def each_source(fn):
        for k, (dr, dc) in enumerate(DIRS):

            @pl.when(inside(row - dr, col - dc))
            def _(k=k):
                fn(k)

    def own_part(t, first, stop):
        def go(c, _):
            b = own[t, pl.ds(c, 3)].reshape(384, 128)
            acc[c] = jnp.dot(e_ref[c], b, preferred_element_type=jnp.float32)
            return 0

        lax.fori_loop(first, stop, go, 0, unroll=stop - first)

    def product(t, c):
        v = [
            jnp.dot(
                eh_ref[side, c],
                halo[t, side, pl.ds(c, 4)].reshape(256, 128),
                preferred_element_type=jnp.float32,
            )
            for side in (0, 1)
        ]
        v = acc[c] + jnp.concatenate(v, axis=0)
        v = v + pltpu.roll(v, RANK, 1)
        return y[c] * diag_ref[c] + mine_ref[c] * v

    def start_stage(t, s, packed):
        place, peers = stages[s]
        gsum[t, s, place] = packed
        for d, there in enumerate(peers):
            pltpu.make_async_remote_copy(
                src_ref=gsum.at[t, s, place],
                dst_ref=gsum.at[t, s, place],
                send_sem=gsend.at[t, s, d],
                recv_sem=grecv.at[t, s, d],
                device_id=there,
                device_id_type=MESH_ID,
            ).start()

    def end_stage(t, s):
        place, peers = stages[s]
        n = len(peers) + 1
        for d, there in enumerate(peers):
            pltpu.make_async_remote_copy(
                src_ref=gsum.at[t, s, place],
                dst_ref=gsum.at[t, s, (place + n - 1 - d) % n],
                send_sem=gsend.at[t, s, d],
                recv_sem=grecv.at[t, s, d],
                device_id=there,
                device_id_type=MESH_ID,
            ).wait_recv()
        packed = gsum[t, s, 0]
        for i in range(1, n):
            packed = packed + gsum[t, s, i]
        return packed

    def new_rows(t, c, v):
        p = pair_of(v, low)
        total[...] += lax.dot_general(p, p, TN, preferred_element_type=jnp.float32)
        if t < ITERS - 1:
            y[c] = v
            own[t + 1, c + 1] = pair_of(v * scale_ref[c], low)
        else:
            pair[c] = p

    def solver(packed):
        gram = jnp.concatenate([packed[:, :64], packed[:, 64:]], axis=0)
        inv = inverse_factor(gram)
        hi = inv.astype(jnp.bfloat16)
        lo = (inv - hi.astype(jnp.float32)).astype(jnp.bfloat16)
        both = jnp.concatenate([hi, hi, lo, lo], axis=1)
        both = jnp.concatenate([both, both], axis=0)

        def solve(p):
            p = jnp.concatenate([p, p], axis=1)
            return lax.dot_general(p, both, NT, preferred_element_type=jnp.float32)

        return solve

    def first(c, _):
        own[0, c + 1] = pair_of(y[c] * scale_ref[c], low)
        return 0

    lax.fori_loop(0, TC, first, 0, unroll=4)
    each_target(lambda k: panel(0, k).start())
    own_part(0, 1, TC - 1)
    each_source(lambda k: panel(0, k).wait_recv())
    own_part(0, 0, 1)
    own_part(0, TC - 1, TC)
    total[...] = jnp.zeros((128, 128), jnp.float32)

    def rows0(c, _):
        new_rows(0, c, product(0, c))
        return 0

    lax.fori_loop(0, TC, rows0, 0, unroll=8)

    solve = None
    for t in range(ITERS):
        g = total[...]
        g = g[:, :64] + g[:, 64:]
        g = g[:64] + g[64:]
        packed = jnp.concatenate([g[:32], g[32:]], axis=1)
        more = t < ITERS - 1
        start_stage(t, 0, packed)
        if more:
            each_target(lambda k: panel(t + 1, k).start())
            own_part(t + 1, 1, 5)
        start_stage(t, 1, end_stage(t, 0))
        if more:
            own_part(t + 1, 5, 10)
        start_stage(t, 2, end_stage(t, 1))
        if more:
            own_part(t + 1, 10, TC - 1)
        start_stage(t, 3, end_stage(t, 2))
        if more:
            each_source(lambda k: panel(t + 1, k).wait_recv())
            own_part(t + 1, 0, 1)
            own_part(t + 1, TC - 1, TC)

            def apply(c, _):
                pair[c] = pair_of(product(t + 1, c), low)
                return 0

            lax.fori_loop(0, TC, apply, 0, unroll=8)
        solve = solver(end_stage(t, 3))
        if more:
            total[...] = jnp.zeros((128, 128), jnp.float32)

            def rows(c, _):
                new_rows(t + 1, c, solve(pair[c]))
                return 0

            lax.fori_loop(0, TC, rows, 0, unroll=8)

    factor = math.sqrt(float(NROW * 2 * NCOL * TC * PATCH))

    def last(c, _):
        y[c] = factor * solve(pair[c])
        for k in (0, 1):
            even = y[c, pl.ds(k * PATCH, PATCH // 2, stride=2)]
            odd = y[c, pl.ds(k * PATCH + 1, PATCH // 2, stride=2)]
            out_ref[k, c] = jnp.where(lane_low[: PATCH // 2], even, odd)
        return 0

    lax.fori_loop(0, TC, last, 0, unroll=4)

    sent()
    for t in range(ITERS):
        each_target(lambda k: panel(t, k).wait_send())
        for s, (place, peers) in enumerate(stages):
            for d, there in enumerate(peers):
                pltpu.make_async_remote_copy(
                    src_ref=gsum.at[t, s, place],
                    dst_ref=gsum.at[t, s, place],
                    send_sem=gsend.at[t, s, d],
                    recv_sem=grecv.at[t, s, d],
                    device_id=there,
                    device_id_type=MESH_ID,
                ).wait_send()


VM = pl.BlockSpec(memory_space=pltpu.VMEM)
DMA = pltpu.SemaphoreType.DMA
LIMIT = 60 * 2**20


def local(features, tissue, probe):
    width = features.shape[-1]
    full = (TC, 128, 128)
    wide = (TC + 2, 128, width)
    out = pl.pallas_call(
        kernel,
        out_shape=jax.ShapeDtypeStruct((2, TC, PATCH // 2, 2 * RANK), jnp.float32),
        in_specs=[pl.BlockSpec(memory_space=pl.ANY), VM, VM],
        out_specs=VM,
        scratch_shapes=[
            pltpu.VMEM(features.shape, jnp.bfloat16),
            pltpu.VMEM(wide, jnp.bfloat16),
            pltpu.VMEM(wide, jnp.bfloat16),
            pltpu.VMEM((4, TC + 2, 8, 128), jnp.float32),
            pltpu.VMEM((TC + 1, 128, 128), jnp.float32),
            pltpu.VMEM((2, TC, PATCH, 256), jnp.bfloat16),
            pltpu.VMEM((TC, 128, 384), jnp.bfloat16),
            pltpu.VMEM((2, TC, PATCH, 256), jnp.bfloat16),
            pltpu.VMEM(full, jnp.float32),
            pltpu.VMEM(full, jnp.float32),
            pltpu.VMEM(full, jnp.float32),
            pltpu.VMEM((ITERS, TC + 2, 128, 128), jnp.bfloat16),
            pltpu.VMEM((ITERS, 2, TC + 3, PATCH, 128), jnp.bfloat16),
            pltpu.VMEM(full, jnp.float32),
            pltpu.VMEM(full, jnp.float32),
            pltpu.VMEM(full, jnp.bfloat16),
            pltpu.VMEM((128, 128), jnp.float32),
            pltpu.VMEM((ITERS, 4, 4, 32, 128), jnp.float32),
            DMA((2, TC + 1)), DMA((2, TC + 1)), DMA((4,)), DMA((4,)), DMA((4,)), DMA((4,)),
            DMA((2, TC + 1)), DMA((2, TC + 1)),
            DMA((ITERS, 8)), DMA((ITERS, 8)), DMA((ITERS, 4, 3)), DMA((ITERS, 4, 3)),
            DMA((TC + 1,)),
        ],
        compiler_params=pltpu.CompilerParams(
            collective_id=0, has_side_effects=True, vmem_limit_bytes=LIMIT
        ),
        name="range_finder",
    )(features, tissue, probe.reshape(2, TC, PATCH // 2, 2 * RANK))
    return out.reshape(2, TC, PATCH * RANK)


def solution(mesh):
    torus = Mesh(mesh.devices.reshape(2, 4, 4, 2, 2), AXES)
    return jax.shard_map(
        local,
        mesh=torus,
        in_specs=(P(ROW, COL, None, None), P(ROW, COL, None), P(ROW, COL, None)),
        out_specs=P(ROW, COL, None),
        check_vma=False,
    )
```

```python
import functools
import math

import jax
import jax.numpy as jnp
from jax import lax
from jax.experimental import pallas as pl
from jax.experimental.pallas import tpu as pltpu
from jax.sharding import Mesh
from jax.sharding import PartitionSpec as P

RANK = 64
ITERS = 3
PATCH = 64
AXES = ("row_0", "row_1", "col_0", "col_1", "col_2")
ROW = ("row_0", "row_1")
COL = ("col_0", "col_1", "col_2")
NROW, NCOL = 8, 16
TC = 16
MESH_ID = pl.DeviceIdType.MESH
AFFINITY_TEMP = 4.0

DIRS = ((-1, 0), (1, 0), (0, -1), (0, 1), (-1, -1), (-1, 1), (1, -1), (1, 1))


def position():
    return tuple(lax.axis_index(a) for a in AXES)


def row_col(pos):
    return pos[0] * 4 + pos[1], pos[2] * 4 + pos[3] * 2 + pos[4]


def device_at(row, col):
    row = jnp.clip(row, 0, NROW - 1)
    col = jnp.clip(col, 0, NCOL - 1)
    return (row // 4, row % 4, col // 4, (col // 2) % 2, col % 2)


def inside(row, col):
    return (row >= 0) & (row < NROW) & (col >= 0) & (col < NCOL)


def barrier(row, col, others):
    sem = pltpu.get_barrier_semaphore()
    for dr, dc in DIRS:

        @pl.when(inside(row + dr, col + dc))
        def _(dr=dr, dc=dc):
            pl.semaphore_signal(
                sem, inc=1, device_id=device_at(row + dr, col + dc), device_id_type=MESH_ID
            )

    for other in others:
        pl.semaphore_signal(sem, inc=1, device_id=other, device_id_type=MESH_ID)
    near = sum(inside(row + dr, col + dc).astype(jnp.int32) for dr, dc in DIRS)
    pl.semaphore_wait(sem, near + len(others))


def send_slices(dr, dc, first=1, count=TC):
    if dc == 0:
        src, dst = pl.ds(first, count), pl.ds(first, count)
    elif dc < 0:
        src, dst = pl.ds(1, 1), pl.ds(TC + 1, 1)
    else:
        src, dst = pl.ds(TC, 1), pl.ds(0, 1)
    return src, dst


def halo_copy(own, halo, dr, dc, send, recv, device, first=1, count=TC):
    src, dst = send_slices(dr, dc, first, count)
    if dr == 0:
        a, b = own.at[src], own.at[dst]
    elif dr < 0:
        a, b = own.at[src, 0:PATCH], halo.at[dst, PATCH : 2 * PATCH]
    else:
        a, b = own.at[src, PATCH : 2 * PATCH], halo.at[dst, 0:PATCH]
    return pltpu.make_async_remote_copy(
        src_ref=a, dst_ref=b, send_sem=send, recv_sem=recv, device_id=device, device_id_type=MESH_ID
    )


def mask_copy(mask, dr, dc, send, recv, device):
    src, dst = send_slices(dr, dc)
    if dr == 0:
        a, b = mask.at[0:2, src], mask.at[0:2, dst]
    elif dr < 0:
        a, b = mask.at[0:1, src], mask.at[3:4, dst]
    else:
        a, b = mask.at[1:2, src], mask.at[2:3, dst]
    return pltpu.make_async_remote_copy(
        src_ref=a, dst_ref=b, send_sem=send, recv_sem=recv, device_id=device, device_id_type=MESH_ID
    )


NT = (((1,), (1,)), ((), ()))
TN = (((0,), (0,)), ((), ()))


def eye(n):
    return lax.broadcasted_iota(jnp.int32, (n, n), 0) == lax.broadcasted_iota(jnp.int32, (n, n), 1)


def affinity(
    row, col, feat, tissue, e_ref, eh_ref, scale_ref, mine_ref, diag_ref, own, halo, mask, deg, served,
    fsend, frecv, csend, crecv, msend, mrecv, rsend, rrecv, ready, meanwhile, load_feat, then,
):
    for k in (2, 3):
        mask[k] = jnp.zeros((TC + 2, 8, 128), jnp.float32)
    for k in (0, 1):
        mask[k, 0] = jnp.zeros((8, 128), jnp.float32)
        mask[k, TC + 1] = jnp.zeros((8, 128), jnp.float32)
        t = tissue[k].astype(jnp.float32)
        t = jnp.concatenate([t, t], axis=1)
        for c in range(TC):
            mask[k, c + 1] = jnp.broadcast_to(t[c : c + 1, :], (8, 128))

    def nothing(c, _):
        for side in (0, 1):
            eh_ref[side, c] = jnp.zeros((PATCH, 256), jnp.bfloat16)
        return 0

    lax.fori_loop(0, TC, nothing, 0, unroll=4)
    ready()

    there = [inside(row - 1, col), inside(row + 1, col)]
    device = [device_at(row - 1, col), device_at(row + 1, col)]

    def tile_copy(side, c):
        return pltpu.make_async_remote_copy(
            src_ref=own.at[c, side * PATCH : (side + 1) * PATCH],
            dst_ref=halo.at[c, (1 - side) * PATCH : (2 - side) * PATCH],
            send_sem=fsend.at[side, c],
            recv_sem=frecv.at[1 - side, c],
            device_id=device[side],
            device_id_type=MESH_ID,
        )

    def tile_arrival(side, c):
        return pltpu.make_async_remote_copy(
            src_ref=own.at[c, side * PATCH : (side + 1) * PATCH],
            dst_ref=halo.at[c, side * PATCH : (side + 1) * PATCH],
            send_sem=fsend.at[side, c],
            recv_sem=frecv.at[side, c],
            device_id=device[side],
            device_id_type=MESH_ID,
        )

    def weights_copy(side, c):
        return pltpu.make_async_remote_copy(
            src_ref=served.at[side, c - 1],
            dst_ref=eh_ref.at[1 - side, c - 1],
            send_sem=rsend.at[side, c],
            recv_sem=rrecv.at[1 - side, c],
            device_id=device[side],
            device_id_type=MESH_ID,
        )

    def weights_arrival(side, c):
        return pltpu.make_async_remote_copy(
            src_ref=served.at[side, c - 1],
            dst_ref=eh_ref.at[side, c - 1],
            send_sem=rsend.at[side, c],
            recv_sem=rrecv.at[side, c],
            device_id=device[side],
            device_id_type=MESH_ID,
        )

    crossing = (row == 3) | (row == 4)
    yields = [row == 4, row == 3]

    def on(side, fn):
        @pl.when(there[side])
        def _():
            fn()

    def early(side, fn):
        @pl.when(there[side] & jnp.logical_not(yields[side]))
        def _():
            fn()

    def normalise(c):
        load_feat(c).wait()
        for k in (0, 1):
            v = feat[k, c - 1].astype(jnp.float32)
            total = jnp.sum(v * v, axis=-1, keepdims=True)
            own[c, k * PATCH : (k + 1) * PATCH] = (v * lax.rsqrt(total + 1e-06)).astype(
                jnp.bfloat16
            )

    def side_copy(k):
        dr, dc = DIRS[k]
        return halo_copy(own, halo, dr, dc, csend.at[k], crecv.at[k], device_at(row, col + dc))

    def side_mask(k):
        dr, dc = DIRS[k]
        return mask_copy(mask, dr, dc, msend.at[k], mrecv.at[k], device_at(row + dr, col + dc))

    for k in range(4):
        dr, dc = DIRS[k]

        @pl.when(inside(row + dr, col + dc))
        def _(k=k):
            side_mask(k).start()

    half = TC // 2
    normalise(1)
    normalise(TC)
    normalise(2)
    for k in (2, 3):

        @pl.when(inside(row, col + DIRS[k][1]))
        def _(k=k):
            side_copy(k).start()

    normalise(TC - 1)
    for side in (0, 1):
        early(side, lambda side=side: (tile_copy(side, 1).start(), tile_copy(side, TC).start()))

    def group(g, _):
        normalise(g + 1)
        normalise(TC - g)
        early(0, lambda: tile_copy(0, TC + 1 - g).start())
        early(1, lambda: tile_copy(1, g).start())
        return 0

    lax.fori_loop(2, half, group, 0)
    early(0, lambda: tile_copy(0, half + 1).start())
    early(1, lambda: (tile_copy(1, half).start(), tile_copy(1, half + 1).start()))

    def arrived(k, fn):
        dr, dc = DIRS[k]

        @pl.when(inside(row - dr, col - dc))
        def _():
            fn()

    def sides():
        for k in (2, 3):
            arrived(k, lambda k=k: (side_mask(k).wait_recv(), side_copy(k).wait_recv()))

    up = [1] + list(range(TC, half, -1))
    down = [TC] + list(range(1, half + 2))

    lane = lax.broadcasted_iota(jnp.int32, (128, 128), 1)
    sub = lax.broadcasted_iota(jnp.int32, (128, 128), 0)
    diagonal = lane == sub
    first = lane[0:1] < PATCH

    def block(c, cc):
        s = lax.dot_general(own[c], own[cc], NT, preferred_element_type=jnp.float32)
        w = jnp.exp(AFFINITY_TEMP * (s - 1.0))
        m = jnp.where(first, mask[0, cc, 0:1], mask[1, cc, 0:1])
        return jnp.where(jnp.broadcast_to(m, (128, 128)) > 0.5, w, 0.0)

    def own_blocks(c):
        total = jnp.zeros((128, 1), jnp.float32)
        for d in range(3):
            w = block(c, c + d - 1)
            total = total + jnp.sum(w, axis=1, keepdims=True)
            if d == 1:
                self_w = jnp.sum(jnp.where(diagonal, w, 0.0), axis=1, keepdims=True)
                diag_ref[c - 1] = jnp.broadcast_to(self_w, (128, 128))
                w = jnp.where(diagonal, 0.0, w)
            e_ref[c - 1, :, d * 128 : (d + 1) * 128] = w.astype(jnp.bfloat16)
        deg[c] = jnp.broadcast_to(total, (128, 128))

    meanwhile()

    def rows_of(left, right, right_mask, c):
        s = lax.dot_general(left, right, NT, preferred_element_type=jnp.float32)
        w = jnp.exp(AFFINITY_TEMP * (s - 1.0))
        m0 = jnp.where(first, mask[right_mask, c - 1, 0:1], mask[right_mask, c, 0:1])
        m1 = mask[right_mask, c + 1, 0:1]
        w0 = jnp.where(jnp.broadcast_to(m0, (PATCH, 128)) > 0.5, w[:, :128], 0.0)
        w1 = jnp.where(jnp.broadcast_to(m1[:, :PATCH], (PATCH, PATCH)) > 0.5, w[:, 128:], 0.0)
        w1 = jnp.concatenate([w1, jnp.zeros((PATCH, PATCH), jnp.float32)], axis=1)
        return jnp.concatenate([w0, w1], axis=1).astype(jnp.bfloat16)

    def near(ref, side, c):
        return ref[pl.ds(c - 1, 3), side * PATCH : (side + 1) * PATCH].reshape(3 * PATCH, -1)

    def serve(side, c, wait=True):
        if wait:
            tile_arrival(side, c).wait_recv()
        left = halo[c, side * PATCH : (side + 1) * PATCH]
        served[side, c - 1] = rows_of(left, near(own, side, c), side, c)
        weights_copy(side, c).start()

    def at_home(side, c):
        left = own[c, side * PATCH : (side + 1) * PATCH]
        eh_ref[side, c - 1] = rows_of(left, near(halo, side, c), 2 + side, c)

    def inner(c, _):
        own_blocks(c)
        return 0

    lax.fori_loop(2, 6, inner, 0)
    @pl.when(crossing)
    def _():
        sides()

    for side, columns in ((0, up), (1, down)):

        @pl.when(yields[side])
        def _(side=side, columns=columns):
            for c in columns:
                tile_copy(side, c).start()

    for k in (0, 1):
        arrived(k, lambda k=k: side_mask(k).wait_recv())
    on(0, lambda: serve(0, 2))
    on(1, lambda: serve(1, TC - 1))

    near_end = (row == 0) | (row == NROW - 1)
    late = near_end & ((col % 4 == 1) | (col % 4 == 2))

    def with_sides():
        @pl.when(jnp.logical_not(crossing))
        def _():
            sides()

        for c in (1, TC):
            for side in (0, 1):
                on(side, lambda side=side, c=c: serve(side, c, c != (1, TC)[side]))
        for c in (1, TC):
            own_blocks(c)

    def arrive(g, _):
        on(0, lambda: serve(0, g + 1))
        on(1, lambda: serve(1, TC - g))

        @pl.when(g == 2)
        def _():
            for side in (0, 1):
                on(side, lambda side=side: (tile_arrival(side, (1, TC)[side]).wait_recv()))

        on(0, lambda: at_home(0, g))
        on(1, lambda: at_home(1, TC + 1 - g))

        @pl.when((g == 5) & jnp.logical_not(late))
        def _():
            with_sides()

        @pl.when(g < 7)
        def _():
            own_blocks(2 * g + 2)
            own_blocks(2 * g + 3)

        return 0

    lax.fori_loop(2, half, arrive, 0)
    on(0, lambda: (serve(0, half + 1), at_home(0, half)))

    @pl.when(late)
    def _():
        with_sides()

    def finish(c):
        eh = jnp.concatenate([eh_ref[0, c - 1], eh_ref[1, c - 1]], axis=0).astype(jnp.float32)
        total = deg[c][:, 0:1] + jnp.sum(eh, axis=1, keepdims=True)
        m = jnp.where(first, mask[0, c, 0:1], mask[1, c, 0:1])
        mine = jnp.sum(jnp.where(diagonal, jnp.broadcast_to(m, (128, 128)), 0.0), axis=1, keepdims=True)
        scale = lax.rsqrt(1.0 + mine * total)
        self_w = diag_ref[c - 1]
        scale_ref[c - 1] = jnp.broadcast_to(scale, (128, 128))
        mine_ref[c - 1] = jnp.broadcast_to(scale * mine, (128, 128))
        diag_ref[c - 1] = 1.0 + (mine * scale * scale) * self_w

    def back(side, columns):
        for c in columns:
            weights_arrival(side, c).wait_recv()

    on(0, lambda: back(0, up))
    on(1, lambda: back(1, down))

    def finish_one(c, _):
        finish(c)
        then(c)
        return 0

    lax.fori_loop(1, TC + 1, finish_one, 0, unroll=4)

    def sent():
        for side, mine, theirs in ((0, up, down), (1, down, up)):

            def go(side=side, mine=mine, theirs=theirs):
                for c in mine:
                    tile_copy(side, c).wait_send()
                for c in theirs:
                    weights_copy(side, c).wait_send()

            on(side, go)
        for k in range(4):
            dr, dc = DIRS[k]

            @pl.when(inside(row + dr, col + dc))
            def _(k=k):
                side_mask(k).wait_send()
                if k >= 2:
                    side_copy(k).wait_send()

    return sent


def stage_peers(pos):
    z = pos[3] * 2 + pos[0]
    core = (pos[4], [(pos[0], pos[1], pos[2], pos[3], 1 - pos[4])])
    x = (pos[1], [(pos[0], (pos[1] + d) % 4, pos[2], pos[3], pos[4]) for d in (1, 2, 3)])
    y = (pos[2], [(pos[0], pos[1], (pos[2] + d) % 4, pos[3], pos[4]) for d in (1, 2, 3)])
    along = [(z + d) % 4 for d in (1, 2, 3)]
    zz = (z, [(q % 2, pos[1], pos[2], q // 2, pos[4]) for q in along])
    return [core, y, x, zz]


def inverse_factor(gram):
    n = RANK
    row_block = 8
    on_diagonal = jnp.where(eye(n), gram, 0.0)
    by_row = lax.rsqrt(jnp.sum(on_diagonal, axis=1, keepdims=True))
    by_lane = lax.rsqrt(jnp.sum(on_diagonal, axis=0, keepdims=True))
    start = jnp.concatenate([gram * by_row * by_lane, jnp.where(eye(n), by_lane, 0.0)], axis=1)
    m = [start[q : q + row_block] for q in range(0, n, row_block)]
    sub = lax.broadcasted_iota(jnp.int32, (row_block, 2 * n), 0)
    for k in range(0, n, 2):
        j, i = divmod(k, row_block)
        left = [jnp.broadcast_to(m[q][:, k : k + 1], (row_block, 2 * n)) for q in range(j, len(m))]
        right = [
            jnp.broadcast_to(m[q][:, k + 1 : k + 2], (row_block, 2 * n)) for q in range(j, len(m))
        ]
        r0, r1 = m[j][i : i + 1], m[j][i + 1 : i + 2]
        a, b, d = left[0][i : i + 1], left[0][i + 1 : i + 2], right[0][i + 1 : i + 2]
        inv = 1.0 / (a * d - b * b)
        u0 = (d * r0 - b * r1) * inv
        u1 = (a * r1 - b * r0) * inv
        second = r1 - (b / a) * r0
        for q in range(j, len(m)):
            new = m[q] - (left[q - j] * u0 + right[q - j] * u1)
            if q == j:
                new = jnp.where(sub > i + 1, new, m[q])
                new = jnp.where(sub == i + 1, second, new)
            m[q] = new
    m = jnp.concatenate(m, axis=0)
    d = jnp.sum(jnp.where(eye(n), m[:, :n], 0.0), axis=1, keepdims=True)
    return m[:, n:] * lax.rsqrt(d)


def pair_of(v, low):
    hi = v.astype(jnp.bfloat16)
    lo = (v - hi.astype(jnp.float32)).astype(jnp.bfloat16)
    return jnp.where(low, hi, lo)


def kernel(
    feat_hbm, tissue, probe, out_ref,
    feat, ufeat, hfeat, mask, deg, served, e_ref, eh_ref, scale_ref, mine_ref, diag_ref,
    own, halo, acc, y, pair, gsum,
    fsend, frecv, csend, crecv, msend, mrecv, rsend, rrecv, psend, precv, gsend, grecv, isem,
):
    def load_feat(c):
        return pltpu.make_async_copy(
            feat_hbm.at[:, pl.ds(c - 1, 1)], feat.at[:, pl.ds(c - 1, 1)], isem.at[c]
        )

    for c in range(1, TC // 2 + 1):
        load_feat(c).start()
        load_feat(TC + 1 - c).start()

    pos = position()
    row, col = row_col(pos)
    stages = stage_peers(pos)
    low = lax.broadcasted_iota(jnp.int32, (128, 128), 1) < RANK
    lane_low = lax.broadcasted_iota(jnp.int32, (PATCH, 128), 1) < RANK
    zero = jnp.zeros((128, 128), jnp.bfloat16)

    def clear(i, _):
        own[i, 0] = zero
        own[i, TC + 1] = zero

        def one(c, _):
            for side in (0, 1):
                halo[i, side, c] = zero[:PATCH]
            return 0

        lax.fori_loop(0, TC + 3, one, 0)
        return 0

    lax.fori_loop(0, ITERS, clear, 0)

    def ready():
        barrier(row, col, [p for _, peers in stages for p in peers])

    def meanwhile():
        def load(c, _):
            for k in (0, 1):
                v = probe[k, c]
                w = pltpu.roll(v, RANK, 1)
                even = lane_low[: PATCH // 2]
                y[c, pl.ds(k * PATCH, PATCH // 2, stride=2)] = jnp.where(even, v, w)
                y[c, pl.ds(k * PATCH + 1, PATCH // 2, stride=2)] = jnp.where(even, w, v)
            return 0

        lax.fori_loop(0, TC, load, 0, unroll=4)

    def then(c):
        own[0, c] = pair_of(y[c - 1] * scale_ref[c - 1], low)

    sent = affinity(
        row, col, feat, tissue, e_ref, eh_ref, scale_ref, mine_ref, diag_ref, ufeat, hfeat, mask,
        deg, served, fsend, frecv, csend, crecv, msend, mrecv, rsend, rrecv, ready, meanwhile, load_feat, then,
    )

    def panel(t, k):
        dr, dc = DIRS[k]
        src, dst = send_slices(dr, dc)
        if dr == 0:
            a, b = own.at[t, src], own.at[t, dst]
        elif dr < 0:
            a, b = own.at[t, src, 0:PATCH], halo.at[t, 1, dst]
        else:
            a, b = own.at[t, src, PATCH : 2 * PATCH], halo.at[t, 0, dst]
        return pltpu.make_async_remote_copy(
            src_ref=a, dst_ref=b, send_sem=psend.at[t, k], recv_sem=precv.at[t, k],
            device_id=device_at(row + dr, col + dc), device_id_type=MESH_ID,
        )

    def each_target(fn):
        for k, (dr, dc) in enumerate(DIRS):

            @pl.when(inside(row + dr, col + dc))
            def _(k=k):
                fn(k)

    def each_source(fn):
        for k, (dr, dc) in enumerate(DIRS):

            @pl.when(inside(row - dr, col - dc))
            def _(k=k):
                fn(k)

    def own_part(t, first, stop):
        def go(c, _):
            b = own[t, pl.ds(c, 3)].reshape(384, 128)
            acc[c] = jnp.dot(e_ref[c], b, preferred_element_type=jnp.float32)
            return 0

        lax.fori_loop(first, stop, go, 0, unroll=stop - first)

    def product(t, c):
        v = [
            jnp.dot(
                eh_ref[side, c],
                halo[t, side, pl.ds(c, 4)].reshape(256, 128),
                preferred_element_type=jnp.float32,
            )
            for side in (0, 1)
        ]
        v = acc[c] + jnp.concatenate(v, axis=0)
        v = v + pltpu.roll(v, RANK, 1)
        return y[c] * diag_ref[c] + mine_ref[c] * v

    def start_stage(t, s, packed):
        place, peers = stages[s]
        gsum[t, s, place] = packed
        for d, there in enumerate(peers):
            pltpu.make_async_remote_copy(
                src_ref=gsum.at[t, s, place],
                dst_ref=gsum.at[t, s, place],
                send_sem=gsend.at[t, s, d],
                recv_sem=grecv.at[t, s, d],
                device_id=there,
                device_id_type=MESH_ID,
            ).start()

    def end_stage(t, s):
        place, peers = stages[s]
        n = len(peers) + 1
        for d, there in enumerate(peers):
            pltpu.make_async_remote_copy(
                src_ref=gsum.at[t, s, place],
                dst_ref=gsum.at[t, s, (place + n - 1 - d) % n],
                send_sem=gsend.at[t, s, d],
                recv_sem=grecv.at[t, s, d],
                device_id=there,
                device_id_type=MESH_ID,
            ).wait_recv()
        packed = gsum[t, s, 0]
        for i in range(1, n):
            packed = packed + gsum[t, s, i]
        return packed

    def new_rows(t, c, v):
        p = pair_of(v, low)
        pair[c] = p
        if t < ITERS - 1:
            y[c] = v
            own[t + 1, c + 1] = pair_of(v * scale_ref[c], low)

    def solver(packed):
        gram = jnp.concatenate([packed[:, :64], packed[:, 64:]], axis=0)
        inv = inverse_factor(gram)
        hi = inv.astype(jnp.bfloat16)
        lo = (inv - hi.astype(jnp.float32)).astype(jnp.bfloat16)
        both = jnp.concatenate([hi, hi, lo, lo], axis=1)
        both = jnp.concatenate([both, both], axis=0)

        def solve(p):
            p = jnp.concatenate([p, p], axis=1)
            return lax.dot_general(p, both, NT, preferred_element_type=jnp.float32)

        return solve

    each_target(lambda k: panel(0, k).start())
    own_part(0, 1, TC - 1)
    each_source(lambda k: panel(0, k).wait_recv())
    own_part(0, 0, 1)
    own_part(0, TC - 1, TC)
    def rows0(c, _):
        new_rows(0, c, product(0, c))
        return 0

    lax.fori_loop(0, TC, rows0, 0, unroll=16)

    solve = None
    for t in range(ITERS):
        p = pair[...].reshape(TC * 128, 128)
        g = lax.dot_general(p, p, TN, preferred_element_type=jnp.float32)
        g = g[:, :64] + g[:, 64:]
        g = g[:64] + g[64:]
        packed = jnp.concatenate([g[:32], g[32:]], axis=1)
        more = t < ITERS - 1
        start_stage(t, 0, packed)
        if more:
            each_target(lambda k: panel(t + 1, k).start())
            own_part(t + 1, 1, 5)
        start_stage(t, 1, end_stage(t, 0))
        if more:
            own_part(t + 1, 5, 10)
        start_stage(t, 2, end_stage(t, 1))
        if more:
            own_part(t + 1, 10, TC - 1)
        start_stage(t, 3, end_stage(t, 2))
        if more:
            each_source(lambda k: panel(t + 1, k).wait_recv())
            own_part(t + 1, 0, 1)
            own_part(t + 1, TC - 1, TC)

            def apply(c, _):
                pair[c] = pair_of(product(t + 1, c), low)
                return 0

            lax.fori_loop(0, TC, apply, 0, unroll=16)
        solve = solver(end_stage(t, 3))
        if more:
            def rows(c, _):
                new_rows(t + 1, c, solve(pair[c]))
                return 0

            lax.fori_loop(0, TC, rows, 0, unroll=16)

    factor = math.sqrt(float(NROW * 2 * NCOL * TC * PATCH))

    def last(c, _):
        y[c] = factor * solve(pair[c])
        for k in (0, 1):
            even = y[c, pl.ds(k * PATCH, PATCH // 2, stride=2)]
            odd = y[c, pl.ds(k * PATCH + 1, PATCH // 2, stride=2)]
            out_ref[k, c] = jnp.where(lane_low[: PATCH // 2], even, odd)
        return 0

    lax.fori_loop(0, TC, last, 0, unroll=8)

    sent()
    for t in range(ITERS):
        each_target(lambda k: panel(t, k).wait_send())
        for s, (place, peers) in enumerate(stages):
            for d, there in enumerate(peers):
                pltpu.make_async_remote_copy(
                    src_ref=gsum.at[t, s, place],
                    dst_ref=gsum.at[t, s, place],
                    send_sem=gsend.at[t, s, d],
                    recv_sem=grecv.at[t, s, d],
                    device_id=there,
                    device_id_type=MESH_ID,
                ).wait_send()


VM = pl.BlockSpec(memory_space=pltpu.VMEM)
DMA = pltpu.SemaphoreType.DMA
LIMIT = 60 * 2**20


def local(features, tissue, probe):
    width = features.shape[-1]
    full = (TC, 128, 128)
    wide = (TC + 2, 128, width)
    out = pl.pallas_call(
        kernel,
        out_shape=jax.ShapeDtypeStruct((2, TC, PATCH // 2, 2 * RANK), jnp.float32),
        in_specs=[pl.BlockSpec(memory_space=pl.ANY), VM, VM],
        out_specs=VM,
        scratch_shapes=[
            pltpu.VMEM(features.shape, jnp.bfloat16),
            pltpu.VMEM(wide, jnp.bfloat16),
            pltpu.VMEM(wide, jnp.bfloat16),
            pltpu.VMEM((4, TC + 2, 8, 128), jnp.float32),
            pltpu.VMEM((TC + 1, 128, 128), jnp.float32),
            pltpu.VMEM((2, TC, PATCH, 256), jnp.bfloat16),
            pltpu.VMEM((TC, 128, 384), jnp.bfloat16),
            pltpu.VMEM((2, TC, PATCH, 256), jnp.bfloat16),
            pltpu.VMEM(full, jnp.float32),
            pltpu.VMEM(full, jnp.float32),
            pltpu.VMEM(full, jnp.float32),
            pltpu.VMEM((ITERS, TC + 2, 128, 128), jnp.bfloat16),
            pltpu.VMEM((ITERS, 2, TC + 3, PATCH, 128), jnp.bfloat16),
            pltpu.VMEM(full, jnp.float32),
            pltpu.VMEM(full, jnp.float32),
            pltpu.VMEM(full, jnp.bfloat16),
            pltpu.VMEM((ITERS, 4, 4, 32, 128), jnp.float32),
            DMA((2, TC + 1)), DMA((2, TC + 1)), DMA((4,)), DMA((4,)), DMA((4,)), DMA((4,)),
            DMA((2, TC + 1)), DMA((2, TC + 1)),
            DMA((ITERS, 8)), DMA((ITERS, 8)), DMA((ITERS, 4, 3)), DMA((ITERS, 4, 3)),
            DMA((TC + 1,)),
        ],
        compiler_params=pltpu.CompilerParams(
            collective_id=0, has_side_effects=True, vmem_limit_bytes=LIMIT
        ),
        name="range_finder",
    )(features, tissue, probe.reshape(2, TC, PATCH // 2, 2 * RANK))
    return out.reshape(2, TC, PATCH * RANK)


def solution(mesh):
    torus = Mesh(mesh.devices.reshape(2, 4, 4, 2, 2), AXES)
    return jax.shard_map(
        local,
        mesh=torus,
        in_specs=(P(ROW, COL, None, None), P(ROW, COL, None), P(ROW, COL, None)),
        out_specs=P(ROW, COL, None),
        check_vma=False,
    )
```

```python
import functools
import math

import jax
import jax.numpy as jnp
from jax import lax
from jax.experimental import pallas as pl
from jax.experimental.pallas import tpu as pltpu
from jax.sharding import Mesh
from jax.sharding import PartitionSpec as P

RANK = 64
ITERS = 3
PATCH = 64
AXES = ("row_0", "row_1", "col_0", "col_1", "col_2")
ROW = ("row_0", "row_1")
COL = ("col_0", "col_1", "col_2")
NROW, NCOL = 8, 16
TC = 16
MESH_ID = pl.DeviceIdType.MESH
AFFINITY_TEMP = 4.0

DIRS = ((-1, 0), (1, 0), (0, -1), (0, 1), (-1, -1), (-1, 1), (1, -1), (1, 1))


def position():
    return tuple(lax.axis_index(a) for a in AXES)


def row_col(pos):
    return pos[0] * 4 + pos[1], pos[2] * 4 + pos[3] * 2 + pos[4]


def device_at(row, col):
    row = jnp.clip(row, 0, NROW - 1)
    col = jnp.clip(col, 0, NCOL - 1)
    return (row // 4, row % 4, col // 4, (col // 2) % 2, col % 2)


def inside(row, col):
    return (row >= 0) & (row < NROW) & (col >= 0) & (col < NCOL)


def barrier(row, col, others):
    sem = pltpu.get_barrier_semaphore()
    for dr, dc in DIRS:

        @pl.when(inside(row + dr, col + dc))
        def _(dr=dr, dc=dc):
            pl.semaphore_signal(
                sem, inc=1, device_id=device_at(row + dr, col + dc), device_id_type=MESH_ID
            )

    for other in others:
        pl.semaphore_signal(sem, inc=1, device_id=other, device_id_type=MESH_ID)
    near = sum(inside(row + dr, col + dc).astype(jnp.int32) for dr, dc in DIRS)
    pl.semaphore_wait(sem, near + len(others))


def send_slices(dr, dc, first=1, count=TC):
    if dc == 0:
        src, dst = pl.ds(first, count), pl.ds(first, count)
    elif dc < 0:
        src, dst = pl.ds(1, 1), pl.ds(TC + 1, 1)
    else:
        src, dst = pl.ds(TC, 1), pl.ds(0, 1)
    return src, dst


def halo_copy(own, halo, dr, dc, send, recv, device, first=1, count=TC):
    src, dst = send_slices(dr, dc, first, count)
    if dr == 0:
        a, b = own.at[src], own.at[dst]
    elif dr < 0:
        a, b = own.at[src, 0:PATCH], halo.at[dst, PATCH : 2 * PATCH]
    else:
        a, b = own.at[src, PATCH : 2 * PATCH], halo.at[dst, 0:PATCH]
    return pltpu.make_async_remote_copy(
        src_ref=a, dst_ref=b, send_sem=send, recv_sem=recv, device_id=device, device_id_type=MESH_ID
    )


def mask_copy(mask, dr, dc, send, recv, device):
    src, dst = send_slices(dr, dc)
    if dr == 0:
        a, b = mask.at[0:2, src], mask.at[0:2, dst]
    elif dr < 0:
        a, b = mask.at[0:1, src], mask.at[3:4, dst]
    else:
        a, b = mask.at[1:2, src], mask.at[2:3, dst]
    return pltpu.make_async_remote_copy(
        src_ref=a, dst_ref=b, send_sem=send, recv_sem=recv, device_id=device, device_id_type=MESH_ID
    )


NT = (((1,), (1,)), ((), ()))
TN = (((0,), (0,)), ((), ()))


def eye(n):
    return lax.broadcasted_iota(jnp.int32, (n, n), 0) == lax.broadcasted_iota(jnp.int32, (n, n), 1)


def affinity(
    row, col, feat, tissue, e_ref, eh_ref, scale_ref, mine_ref, diag_ref, own, halo, mask, deg, served,
    fsend, frecv, csend, crecv, msend, mrecv, rsend, rrecv, ready, meanwhile, load_feat, then,
):
    for k in (2, 3):
        mask[k] = jnp.zeros((TC + 2, 8, 128), jnp.float32)
    for k in (0, 1):
        mask[k, 0] = jnp.zeros((8, 128), jnp.float32)
        mask[k, TC + 1] = jnp.zeros((8, 128), jnp.float32)
        t = tissue[k].astype(jnp.float32)
        t = jnp.concatenate([t, t], axis=1)
        for c in range(TC):
            mask[k, c + 1] = jnp.broadcast_to(t[c : c + 1, :], (8, 128))

    def nothing(c, _):
        for side in (0, 1):
            eh_ref[side, c] = jnp.zeros((PATCH, 256), jnp.bfloat16)
        return 0

    lax.fori_loop(0, TC, nothing, 0, unroll=4)
    ready()

    there = [inside(row - 1, col), inside(row + 1, col)]
    device = [device_at(row - 1, col), device_at(row + 1, col)]

    def tile_copy(side, c):
        return pltpu.make_async_remote_copy(
            src_ref=own.at[c, side * PATCH : (side + 1) * PATCH],
            dst_ref=halo.at[c, (1 - side) * PATCH : (2 - side) * PATCH],
            send_sem=fsend.at[side, c],
            recv_sem=frecv.at[1 - side, c],
            device_id=device[side],
            device_id_type=MESH_ID,
        )

    def tile_arrival(side, c):
        return pltpu.make_async_remote_copy(
            src_ref=own.at[c, side * PATCH : (side + 1) * PATCH],
            dst_ref=halo.at[c, side * PATCH : (side + 1) * PATCH],
            send_sem=fsend.at[side, c],
            recv_sem=frecv.at[side, c],
            device_id=device[side],
            device_id_type=MESH_ID,
        )

    def weights_copy(side, c):
        return pltpu.make_async_remote_copy(
            src_ref=served.at[side, c - 1],
            dst_ref=eh_ref.at[1 - side, c - 1],
            send_sem=rsend.at[side, c],
            recv_sem=rrecv.at[1 - side, c],
            device_id=device[side],
            device_id_type=MESH_ID,
        )

    def weights_arrival(side, c):
        return pltpu.make_async_remote_copy(
            src_ref=served.at[side, c - 1],
            dst_ref=eh_ref.at[side, c - 1],
            send_sem=rsend.at[side, c],
            recv_sem=rrecv.at[side, c],
            device_id=device[side],
            device_id_type=MESH_ID,
        )

    crossing = (row == 3) | (row == 4)
    yields = [row == 4, row == 3]

    def on(side, fn):
        @pl.when(there[side])
        def _():
            fn()

    def early(side, fn):
        @pl.when(there[side] & jnp.logical_not(yields[side]))
        def _():
            fn()

    def normalise(c):
        load_feat(c).wait()
        for k in (0, 1):
            v = feat[k, c - 1].astype(jnp.float32)
            total = jnp.sum(v * v, axis=-1, keepdims=True)
            own[c, k * PATCH : (k + 1) * PATCH] = (v * lax.rsqrt(total + 1e-06)).astype(
                jnp.bfloat16
            )

    def side_copy(k):
        dr, dc = DIRS[k]
        return halo_copy(own, halo, dr, dc, csend.at[k], crecv.at[k], device_at(row, col + dc))

    def side_mask(k):
        dr, dc = DIRS[k]
        return mask_copy(mask, dr, dc, msend.at[k], mrecv.at[k], device_at(row + dr, col + dc))

    for k in range(4):
        dr, dc = DIRS[k]

        @pl.when(inside(row + dr, col + dc))
        def _(k=k):
            side_mask(k).start()

    half = TC // 2
    normalise(1)
    normalise(TC)
    normalise(2)
    for k in (2, 3):

        @pl.when(inside(row, col + DIRS[k][1]))
        def _(k=k):
            side_copy(k).start()

    normalise(TC - 1)
    for side in (0, 1):
        early(side, lambda side=side: (tile_copy(side, 1).start(), tile_copy(side, TC).start()))

    def group(g, _):
        normalise(g + 1)
        normalise(TC - g)
        early(0, lambda: tile_copy(0, TC + 1 - g).start())
        early(1, lambda: tile_copy(1, g).start())
        return 0

    lax.fori_loop(2, half, group, 0)
    early(0, lambda: tile_copy(0, half + 1).start())
    early(1, lambda: (tile_copy(1, half).start(), tile_copy(1, half + 1).start()))

    def arrived(k, fn):
        dr, dc = DIRS[k]

        @pl.when(inside(row - dr, col - dc))
        def _():
            fn()

    def sides():
        for k in (2, 3):
            arrived(k, lambda k=k: (side_mask(k).wait_recv(), side_copy(k).wait_recv()))

    up = [1] + list(range(TC, half, -1))
    down = [TC] + list(range(1, half + 2))

    lane = lax.broadcasted_iota(jnp.int32, (128, 128), 1)
    sub = lax.broadcasted_iota(jnp.int32, (128, 128), 0)
    diagonal = lane == sub
    first = lane[0:1] < PATCH

    def block(c, cc):
        s = lax.dot_general(own[c], own[cc], NT, preferred_element_type=jnp.float32)
        w = jnp.exp(AFFINITY_TEMP * (s - 1.0))
        m = jnp.where(first, mask[0, cc, 0:1], mask[1, cc, 0:1])
        return jnp.where(jnp.broadcast_to(m, (128, 128)) > 0.5, w, 0.0)

    def own_blocks(c):
        total = jnp.zeros((128, 1), jnp.float32)
        for d in range(3):
            w = block(c, c + d - 1)
            total = total + jnp.sum(w, axis=1, keepdims=True)
            if d == 1:
                self_w = jnp.sum(jnp.where(diagonal, w, 0.0), axis=1, keepdims=True)
                diag_ref[c - 1] = jnp.broadcast_to(self_w, (128, 128))
                w = jnp.where(diagonal, 0.0, w)
            e_ref[c - 1, :, d * 128 : (d + 1) * 128] = w.astype(jnp.bfloat16)
        deg[c] = jnp.broadcast_to(total, (128, 128))

    meanwhile()

    def rows_of(left, right, right_mask, c):
        s = lax.dot_general(left, right, NT, preferred_element_type=jnp.float32)
        w = jnp.exp(AFFINITY_TEMP * (s - 1.0))
        m0 = jnp.where(first, mask[right_mask, c - 1, 0:1], mask[right_mask, c, 0:1])
        m1 = mask[right_mask, c + 1, 0:1]
        w0 = jnp.where(jnp.broadcast_to(m0, (PATCH, 128)) > 0.5, w[:, :128], 0.0)
        w1 = jnp.where(jnp.broadcast_to(m1[:, :PATCH], (PATCH, PATCH)) > 0.5, w[:, 128:], 0.0)
        w1 = jnp.concatenate([w1, jnp.zeros((PATCH, PATCH), jnp.float32)], axis=1)
        return jnp.concatenate([w0, w1], axis=1).astype(jnp.bfloat16)

    def near(ref, side, c):
        return ref[pl.ds(c - 1, 3), side * PATCH : (side + 1) * PATCH].reshape(3 * PATCH, -1)

    def serve(side, c, wait=True):
        if wait:
            tile_arrival(side, c).wait_recv()
        left = halo[c, side * PATCH : (side + 1) * PATCH]
        served[side, c - 1] = rows_of(left, near(own, side, c), side, c)
        weights_copy(side, c).start()

    def at_home(side, c):
        left = own[c, side * PATCH : (side + 1) * PATCH]
        eh_ref[side, c - 1] = rows_of(left, near(halo, side, c), 2 + side, c)

    def inner(c, _):
        own_blocks(c)
        return 0

    lax.fori_loop(2, 6, inner, 0)
    @pl.when(crossing)
    def _():
        sides()

    for side, columns in ((0, up), (1, down)):

        @pl.when(yields[side])
        def _(side=side, columns=columns):
            for c in columns:
                tile_copy(side, c).start()

    for k in (0, 1):
        arrived(k, lambda k=k: side_mask(k).wait_recv())
    on(0, lambda: serve(0, 2))
    on(1, lambda: serve(1, TC - 1))

    def arrive(g, _):
        on(0, lambda: serve(0, g + 1))
        on(1, lambda: serve(1, TC - g))

        @pl.when(g == 2)
        def _():
            for side in (0, 1):
                on(side, lambda side=side: (tile_arrival(side, (1, TC)[side]).wait_recv()))

        on(0, lambda: at_home(0, g))
        on(1, lambda: at_home(1, TC + 1 - g))

        @pl.when(g < 7)
        def _():
            own_blocks(2 * g + 2)
            own_blocks(2 * g + 3)

        return 0

    lax.fori_loop(2, half, arrive, 0)
    on(0, lambda: (serve(0, half + 1), at_home(0, half)))

    @pl.when(jnp.logical_not(crossing))
    def _():
        sides()

    for c in (1, TC):
        for side in (0, 1):
            on(side, lambda side=side, c=c: serve(side, c, c != (1, TC)[side]))
    for c in (1, TC):
        own_blocks(c)

    def finish(c):
        eh = jnp.concatenate([eh_ref[0, c - 1], eh_ref[1, c - 1]], axis=0).astype(jnp.float32)
        total = deg[c][:, 0:1] + jnp.sum(eh, axis=1, keepdims=True)
        m = jnp.where(first, mask[0, c, 0:1], mask[1, c, 0:1])
        mine = jnp.sum(jnp.where(diagonal, jnp.broadcast_to(m, (128, 128)), 0.0), axis=1, keepdims=True)
        scale = lax.rsqrt(1.0 + mine * total)
        self_w = diag_ref[c - 1]
        scale_ref[c - 1] = jnp.broadcast_to(scale, (128, 128))
        mine_ref[c - 1] = jnp.broadcast_to(scale * mine, (128, 128))
        diag_ref[c - 1] = 1.0 + (mine * scale * scale) * self_w

    def back(side, columns):
        for c in columns:
            weights_arrival(side, c).wait_recv()

    on(0, lambda: back(0, up))
    on(1, lambda: back(1, down))

    def finish_one(c, _):
        finish(c)
        then(c)
        return 0

    lax.fori_loop(1, TC + 1, finish_one, 0, unroll=4)

    def sent():
        for side, mine, theirs in ((0, up, down), (1, down, up)):

            def go(side=side, mine=mine, theirs=theirs):
                for c in mine:
                    tile_copy(side, c).wait_send()
                for c in theirs:
                    weights_copy(side, c).wait_send()

            on(side, go)
        for k in range(4):
            dr, dc = DIRS[k]

            @pl.when(inside(row + dr, col + dc))
            def _(k=k):
                side_mask(k).wait_send()
                if k >= 2:
                    side_copy(k).wait_send()

    return sent


def stage_peers(pos):
    z = pos[3] * 2 + pos[0]
    core = (pos[4], [(pos[0], pos[1], pos[2], pos[3], 1 - pos[4])])
    x = (pos[1], [(pos[0], (pos[1] + d) % 4, pos[2], pos[3], pos[4]) for d in (1, 2, 3)])
    y = (pos[2], [(pos[0], pos[1], (pos[2] + d) % 4, pos[3], pos[4]) for d in (1, 2, 3)])
    along = [(z + d) % 4 for d in (1, 2, 3)]
    zz = (z, [(q % 2, pos[1], pos[2], q // 2, pos[4]) for q in along])
    return [core, y, x, zz]


def inverse_factor(gram):
    n = RANK
    row_block = 8
    on_diagonal = jnp.where(eye(n), gram, 0.0)
    by_row = lax.rsqrt(jnp.sum(on_diagonal, axis=1, keepdims=True))
    by_lane = lax.rsqrt(jnp.sum(on_diagonal, axis=0, keepdims=True))
    start = jnp.concatenate([gram * by_row * by_lane, jnp.where(eye(n), by_lane, 0.0)], axis=1)
    m = [start[q : q + row_block] for q in range(0, n, row_block)]
    sub = lax.broadcasted_iota(jnp.int32, (row_block, 2 * n), 0)
    for k in range(0, n, 2):
        j, i = divmod(k, row_block)
        left = [jnp.broadcast_to(m[q][:, k : k + 1], (row_block, 2 * n)) for q in range(j, len(m))]
        right = [
            jnp.broadcast_to(m[q][:, k + 1 : k + 2], (row_block, 2 * n)) for q in range(j, len(m))
        ]
        r0, r1 = m[j][i : i + 1], m[j][i + 1 : i + 2]
        a, b, d = left[0][i : i + 1], left[0][i + 1 : i + 2], right[0][i + 1 : i + 2]
        inv = 1.0 / (a * d - b * b)
        u0 = (d * r0 - b * r1) * inv
        u1 = (a * r1 - b * r0) * inv
        second = r1 - (b / a) * r0
        for q in range(j, len(m)):
            new = m[q] - (left[q - j] * u0 + right[q - j] * u1)
            if q == j:
                new = jnp.where(sub > i + 1, new, m[q])
                new = jnp.where(sub == i + 1, second, new)
            m[q] = new
    m = jnp.concatenate(m, axis=0)
    d = jnp.sum(jnp.where(eye(n), m[:, :n], 0.0), axis=1, keepdims=True)
    return m[:, n:] * lax.rsqrt(d)


def pair_of(v, low):
    hi = v.astype(jnp.bfloat16)
    lo = (v - hi.astype(jnp.float32)).astype(jnp.bfloat16)
    return jnp.where(low, hi, lo)


def kernel(
    feat_hbm, tissue, probe, out_ref,
    feat, ufeat, hfeat, mask, deg, served, e_ref, eh_ref, scale_ref, mine_ref, diag_ref,
    own, halo, acc, y, pair, gsum,
    fsend, frecv, csend, crecv, msend, mrecv, rsend, rrecv, psend, precv, gsend, grecv, isem,
):
    def load_feat(c):
        return pltpu.make_async_copy(
            feat_hbm.at[:, pl.ds(c - 1, 1)], feat.at[:, pl.ds(c - 1, 1)], isem.at[c]
        )

    for c in range(1, TC // 2 + 1):
        load_feat(c).start()
        load_feat(TC + 1 - c).start()

    pos = position()
    row, col = row_col(pos)
    stages = stage_peers(pos)
    low = lax.broadcasted_iota(jnp.int32, (128, 128), 1) < RANK
    lane_low = lax.broadcasted_iota(jnp.int32, (PATCH, 128), 1) < RANK
    zero = jnp.zeros((128, 128), jnp.bfloat16)

    def clear(i, _):
        own[i, 0] = zero
        own[i, TC + 1] = zero

        def one(c, _):
            for side in (0, 1):
                halo[i, side, c] = zero[:PATCH]
            return 0

        lax.fori_loop(0, TC + 3, one, 0)
        return 0

    lax.fori_loop(0, ITERS, clear, 0)

    def ready():
        barrier(row, col, [p for _, peers in stages for p in peers])

    def meanwhile():
        def load(c, _):
            for k in (0, 1):
                v = probe[k, c]
                w = pltpu.roll(v, RANK, 1)
                even = lane_low[: PATCH // 2]
                y[c, pl.ds(k * PATCH, PATCH // 2, stride=2)] = jnp.where(even, v, w)
                y[c, pl.ds(k * PATCH + 1, PATCH // 2, stride=2)] = jnp.where(even, w, v)
            return 0

        lax.fori_loop(0, TC, load, 0, unroll=4)

    def then(c):
        own[0, c] = pair_of(y[c - 1] * scale_ref[c - 1], low)

    sent = affinity(
        row, col, feat, tissue, e_ref, eh_ref, scale_ref, mine_ref, diag_ref, ufeat, hfeat, mask,
        deg, served, fsend, frecv, csend, crecv, msend, mrecv, rsend, rrecv, ready, meanwhile, load_feat, then,
    )

    def panel(t, k):
        dr, dc = DIRS[k]
        src, dst = send_slices(dr, dc)
        if dr == 0:
            a, b = own.at[t, src], own.at[t, dst]
        elif dr < 0:
            a, b = own.at[t, src, 0:PATCH], halo.at[t, 1, dst]
        else:
            a, b = own.at[t, src, PATCH : 2 * PATCH], halo.at[t, 0, dst]
        return pltpu.make_async_remote_copy(
            src_ref=a, dst_ref=b, send_sem=psend.at[t, k], recv_sem=precv.at[t, k],
            device_id=device_at(row + dr, col + dc), device_id_type=MESH_ID,
        )

    def each_target(fn):
        for k, (dr, dc) in enumerate(DIRS):

            @pl.when(inside(row + dr, col + dc))
            def _(k=k):
                fn(k)

    def each_source(fn):
        for k, (dr, dc) in enumerate(DIRS):

            @pl.when(inside(row - dr, col - dc))
            def _(k=k):
                fn(k)

    def own_part(t, first, stop):
        def go(c, _):
            b = own[t, pl.ds(c, 3)].reshape(384, 128)
            acc[c] = jnp.dot(e_ref[c], b, preferred_element_type=jnp.float32)
            return 0

        lax.fori_loop(first, stop, go, 0, unroll=stop - first)

    def product(t, c):
        v = [
            jnp.dot(
                eh_ref[side, c],
                halo[t, side, pl.ds(c, 4)].reshape(256, 128),
                preferred_element_type=jnp.float32,
            )
            for side in (0, 1)
        ]
        v = acc[c] + jnp.concatenate(v, axis=0)
        v = v + pltpu.roll(v, RANK, 1)
        return y[c] * diag_ref[c] + mine_ref[c] * v

    def start_stage(t, s, packed):
        place, peers = stages[s]
        gsum[t, s, place] = packed
        for d, there in enumerate(peers):
            pltpu.make_async_remote_copy(
                src_ref=gsum.at[t, s, place],
                dst_ref=gsum.at[t, s, place],
                send_sem=gsend.at[t, s, d],
                recv_sem=grecv.at[t, s, d],
                device_id=there,
                device_id_type=MESH_ID,
            ).start()

    def end_stage(t, s):
        place, peers = stages[s]
        n = len(peers) + 1
        for d, there in enumerate(peers):
            pltpu.make_async_remote_copy(
                src_ref=gsum.at[t, s, place],
                dst_ref=gsum.at[t, s, (place + n - 1 - d) % n],
                send_sem=gsend.at[t, s, d],
                recv_sem=grecv.at[t, s, d],
                device_id=there,
                device_id_type=MESH_ID,
            ).wait_recv()
        packed = gsum[t, s, 0]
        for i in range(1, n):
            packed = packed + gsum[t, s, i]
        return packed

    def new_rows(t, c, v):
        p = pair_of(v, low)
        pair[c] = p
        if t < ITERS - 1:
            y[c] = v
            own[t + 1, c + 1] = pair_of(v * scale_ref[c], low)

    def solver(packed):
        gram = jnp.concatenate([packed[:, :64], packed[:, 64:]], axis=0)
        inv = inverse_factor(gram)
        hi = inv.astype(jnp.bfloat16)
        lo = (inv - hi.astype(jnp.float32)).astype(jnp.bfloat16)
        both = jnp.concatenate([hi, hi, lo, lo], axis=1)
        both = jnp.concatenate([both, both], axis=0)

        def solve(p):
            p = jnp.concatenate([p, p], axis=1)
            return lax.dot_general(p, both, NT, preferred_element_type=jnp.float32)

        return solve

    each_target(lambda k: panel(0, k).start())
    own_part(0, 1, TC - 1)
    each_source(lambda k: panel(0, k).wait_recv())
    own_part(0, 0, 1)
    own_part(0, TC - 1, TC)
    def rows0(c, _):
        new_rows(0, c, product(0, c))
        return 0

    lax.fori_loop(0, TC, rows0, 0, unroll=16)

    solve = None
    for t in range(ITERS):
        p = pair[...].reshape(TC * 128, 128)
        g = lax.dot_general(p, p, TN, preferred_element_type=jnp.float32)
        g = g[:, :64] + g[:, 64:]
        g = g[:64] + g[64:]
        packed = jnp.concatenate([g[:32], g[32:]], axis=1)
        more = t < ITERS - 1
        start_stage(t, 0, packed)
        if more:
            each_target(lambda k: panel(t + 1, k).start())
            own_part(t + 1, 1, 5)
        start_stage(t, 1, end_stage(t, 0))
        if more:
            own_part(t + 1, 5, 10)
        start_stage(t, 2, end_stage(t, 1))
        if more:
            own_part(t + 1, 10, TC - 1)
        start_stage(t, 3, end_stage(t, 2))
        if more:
            each_source(lambda k: panel(t + 1, k).wait_recv())
            own_part(t + 1, 0, 1)
            own_part(t + 1, TC - 1, TC)

            def apply(c, _):
                pair[c] = pair_of(product(t + 1, c), low)
                return 0

            lax.fori_loop(0, TC, apply, 0, unroll=16)
        solve = solver(end_stage(t, 3))
        if more:
            def rows(c, _):
                new_rows(t + 1, c, solve(pair[c]))
                return 0

            lax.fori_loop(0, TC, rows, 0, unroll=16)

    factor = math.sqrt(float(NROW * 2 * NCOL * TC * PATCH))

    def last(c, _):
        y[c] = factor * solve(pair[c])
        for k in (0, 1):
            even = y[c, pl.ds(k * PATCH, PATCH // 2, stride=2)]
            odd = y[c, pl.ds(k * PATCH + 1, PATCH // 2, stride=2)]
            out_ref[k, c] = jnp.where(lane_low[: PATCH // 2], even, odd)
        return 0

    lax.fori_loop(0, TC, last, 0, unroll=8)

    sent()
    for t in range(ITERS):
        each_target(lambda k: panel(t, k).wait_send())
        for s, (place, peers) in enumerate(stages):
            for d, there in enumerate(peers):
                pltpu.make_async_remote_copy(
                    src_ref=gsum.at[t, s, place],
                    dst_ref=gsum.at[t, s, place],
                    send_sem=gsend.at[t, s, d],
                    recv_sem=grecv.at[t, s, d],
                    device_id=there,
                    device_id_type=MESH_ID,
                ).wait_send()


VM = pl.BlockSpec(memory_space=pltpu.VMEM)
DMA = pltpu.SemaphoreType.DMA
LIMIT = 60 * 2**20


def local(features, tissue, probe):
    width = features.shape[-1]
    full = (TC, 128, 128)
    wide = (TC + 2, 128, width)
    out = pl.pallas_call(
        kernel,
        out_shape=jax.ShapeDtypeStruct((2, TC, PATCH // 2, 2 * RANK), jnp.float32),
        in_specs=[pl.BlockSpec(memory_space=pl.ANY), VM, VM],
        out_specs=VM,
        scratch_shapes=[
            pltpu.VMEM(features.shape, jnp.bfloat16),
            pltpu.VMEM(wide, jnp.bfloat16),
            pltpu.VMEM(wide, jnp.bfloat16),
            pltpu.VMEM((4, TC + 2, 8, 128), jnp.float32),
            pltpu.VMEM((TC + 1, 128, 128), jnp.float32),
            pltpu.VMEM((2, TC, PATCH, 256), jnp.bfloat16),
            pltpu.VMEM((TC, 128, 384), jnp.bfloat16),
            pltpu.VMEM((2, TC, PATCH, 256), jnp.bfloat16),
            pltpu.VMEM(full, jnp.float32),
            pltpu.VMEM(full, jnp.float32),
            pltpu.VMEM(full, jnp.float32),
            pltpu.VMEM((ITERS, TC + 2, 128, 128), jnp.bfloat16),
            pltpu.VMEM((ITERS, 2, TC + 3, PATCH, 128), jnp.bfloat16),
            pltpu.VMEM(full, jnp.float32),
            pltpu.VMEM(full, jnp.float32),
            pltpu.VMEM(full, jnp.bfloat16),
            pltpu.VMEM((ITERS, 4, 4, 32, 128), jnp.float32),
            DMA((2, TC + 1)), DMA((2, TC + 1)), DMA((4,)), DMA((4,)), DMA((4,)), DMA((4,)),
            DMA((2, TC + 1)), DMA((2, TC + 1)),
            DMA((ITERS, 8)), DMA((ITERS, 8)), DMA((ITERS, 4, 3)), DMA((ITERS, 4, 3)),
            DMA((TC + 1,)),
        ],
        compiler_params=pltpu.CompilerParams(
            collective_id=0, has_side_effects=True, vmem_limit_bytes=LIMIT
        ),
        name="range_finder",
    )(features, tissue, probe.reshape(2, TC, PATCH // 2, 2 * RANK))
    return out.reshape(2, TC, PATCH * RANK)


def solution(mesh):
    torus = Mesh(mesh.devices.reshape(2, 4, 4, 2, 2), AXES)
    return jax.shard_map(
        local,
        mesh=torus,
        in_specs=(P(ROW, COL, None, None), P(ROW, COL, None), P(ROW, COL, None)),
        out_specs=P(ROW, COL, None),
        check_vma=False,
    )
```
